128 devices in a mesh: rows: 64 (over y, z, x), rep: 2 (over core).
Axes of the slice: x: 4, y: 4, z: 4, core: 2. Of those that a mesh axis runs over, the one named last changes fastest.
Arguments:
- margin_blocks: float32 [256, 16, 128, 128], P('rows', 'rep'), may hold values from -1 to 1
- margin_cols: int32 [256, 16], P('rows', 'rep'), may hold values from 0 to 255, as said below
- factor_blocks: float32 [256, 16, 128, 128], P('rows'), may hold values from -0.5 to 0.5
- factor_cols: int32 [256, 16], P('rows'), may hold values from 0 to 255, as said below
- product_cols: int32 [256, 24], P('rows'), may hold values from 0 to 255, as said below
- metric_cols: int32 [256, 24], P('rows'), may hold values from 0 to 255, as said below
Outputs:
- product: float32 [256, 24, 128, 128], P('rows', 'rep')
- metric: float32 [256, 24, 128, 128], P('rows', 'rep')
The draws below stay inside these ranges and needn't reach their ends.
Inputs may be any that keep to these rules, and one draw needn't show every extreme that they name: `margin_cols`: each block row holds 16 distinct block columns, its own index among them, each within 8 of the row index cyclically modulo 256. `factor_cols`: each block row holds 16 distinct block columns, each in the block rows of an index of rows at most 2 away from the row's own (column // 4 against row // 4, cyclically); every block column is named by exactly 16 block rows. `product_cols`: each block row holds 24 distinct block columns, its own index among them, each within 16 of the row index cyclically. `metric_cols`: each block row holds 24 distinct block columns, its own index among them, each within 16 of the row index cyclically.
All inputs are finite; a program needn't handle non-finite values.
Results may differ from the reference program's by a relative error of at most 0.0003.
Values sent between devices are 32-bit elements; how exact they have to be, the bound alone decides.
No kernel may reach another device: no remote copies, remote signals or barrier semaphores. Data moves between devices by JAX's collectives and lax.ppermute only.
A program may use at most 192 MiB of HBM per device.

```python
import jax
import jax.numpy as jnp
from jax import lax

BLOCK = 128
ROWS_DEV = 4
SLOTS_S = 16
SLOTS_Z = 16
SLOTS_Y = 24
SLOTS_X = 24
BLOCKS = 256


def band_pattern(key, count, reach):
    span = 2 * reach + 1
    scores = jax.random.randint(key, (BLOCKS, span), 0, 1 << 20) * span + jnp.arange(span, dtype=jnp.int32)[None, :]
    scores = scores.at[:, reach].set(jnp.int32(1 << 30))
    chosen_values, chosen_offsets = lax.top_k(scores, count)
    row_index = jnp.arange(BLOCKS, dtype=jnp.int32)[:, None]
    return ((row_index + chosen_offsets.astype(jnp.int32) - reach) % BLOCKS).astype(jnp.int32)


def draw_margin_cols(key, part):
    return band_pattern(jax.random.fold_in(key, 11), SLOTS_S, 2 * ROWS_DEV)


def draw_product_cols(key, part):
    return band_pattern(jax.random.fold_in(key, 12), SLOTS_Y, 4 * ROWS_DEV)


def draw_metric_cols(key, part):
    return band_pattern(jax.random.fold_in(key, 13), SLOTS_X, 4 * ROWS_DEV)


def random_orders(key, groups):
    scores = jax.random.randint(key, (groups, 5, ROWS_DEV), 0, 1 << 20) * ROWS_DEV + jnp.arange(ROWS_DEV, dtype=jnp.int32)
    return jnp.argsort(scores, axis=-1, stable=True).astype(jnp.int32)


def draw_factor_cols(key, part):
    groups = BLOCKS // ROWS_DEV
    key = jax.random.fold_in(key, 14)
    key_counts, key_subset, key_place, key_shift = jax.random.split(key, 4)
    even_counts = SLOTS_Z // 5 + (jnp.arange(5) < SLOTS_Z % 5).astype(jnp.int32)
    counts = even_counts[jax.random.permutation(key_counts, 5)]
    bounds = jnp.cumsum(counts)
    starts = bounds - counts
    slot_index = jnp.arange(SLOTS_Z, dtype=jnp.int32)
    band_index = jnp.sum((slot_index[:, None] >= bounds[None, :]).astype(jnp.int32), axis=1)
    within = slot_index - starts[band_index]
    subset_order = random_orders(key_subset, groups)
    place_order = random_orders(key_place, groups)
    shift_order = random_orders(key_shift, groups)
    row_index = jnp.arange(BLOCKS, dtype=jnp.int32)
    group_index = (row_index // ROWS_DEV)[:, None]
    inner_index = (row_index % ROWS_DEV)[:, None]
    chosen_shift = subset_order[group_index, band_index[None, :], within[None, :]]
    start_shift = shift_order[group_index, band_index[None, :], inner_index]
    target_place = place_order[group_index, band_index[None, :], (start_shift + chosen_shift) % ROWS_DEV]
    target_group = (group_index + band_index[None, :] - 2) % groups
    return (target_group * ROWS_DEV + target_place).astype(jnp.int32)


def shard_levels(key, shape, shards, smallest, top_value):
    def one(dim, blocks):
        draws = jax.random.uniform(jax.random.fold_in(jax.random.fold_in(key, 6), dim), (blocks,), jnp.float32, smallest / len(shards), top_value / len(shards))
        return jnp.repeat(jnp.exp(draws), shape[dim] // blocks).reshape((-1,) + (1,) * (len(shape) - dim - 1))

    gain = one(*shards[0])
    for cut in shards[1:]:
        gain = gain * one(*cut)
    return gain


def noise(rng, shape, scale, bound, pieces=(), kind=jnp.bfloat16):
    array = scale * jax.random.normal(rng, shape, jnp.float32)
    if pieces:
        array = array * shard_levels(rng, shape, pieces, -0.22, 0.18)
    return jnp.clip(array, -bound, bound).astype(kind)


def setup_inputs(seed: int = 0) -> dict:
    splits = jax.random.split(jax.random.key(seed), 7)
    margin_blocks = noise(splits[0], (BLOCKS, SLOTS_S, BLOCK, BLOCK), (BLOCK // 4) ** -0.5, 1.0, ((0, 64), (1, 2)), jnp.float32)
    margin_cols = draw_margin_cols(jax.random.fold_in(splits[6], 71), 0)
    factor_blocks = noise(splits[2], (BLOCKS, SLOTS_Z, BLOCK, BLOCK), BLOCK ** -0.5, 0.5, ((0, 64),), jnp.float32)
    factor_cols = draw_factor_cols(jax.random.fold_in(splits[6], 71), 0)
    product_cols = draw_product_cols(jax.random.fold_in(splits[6], 71), 0)
    metric_cols = draw_metric_cols(jax.random.fold_in(splits[6], 71), 0)
    return dict(margin_blocks=margin_blocks, margin_cols=margin_cols, factor_blocks=factor_blocks, factor_cols=factor_cols, product_cols=product_cols, metric_cols=metric_cols)


HIGHEST = lax.Precision.HIGHEST


def reference(margin_blocks, margin_cols, factor_blocks, factor_cols, product_cols, metric_cols):
    def product_row(packed):
        margin_row, column_row, kept_row = packed
        picked = factor_blocks[column_row]
        partial_terms = jnp.einsum('kab,kmbc->kmac', margin_row, picked, precision=HIGHEST)
        selector = (factor_cols[column_row][:, :, None] == kept_row[None, None, :]).astype(jnp.float32)
        return jnp.einsum('kmy,kmac->yac', selector, partial_terms, precision=HIGHEST)

    product = lax.map(product_row, (margin_blocks, margin_cols, product_cols))
    flat_cols = factor_cols.reshape(-1)
    flat_blocks = factor_blocks.reshape(-1, BLOCK, BLOCK)

    def metric_row(packed):
        target, kept_row = packed
        positions = jnp.nonzero(flat_cols == target, size=SLOTS_Z)[0].astype(jnp.int32)
        source_rows = (positions // SLOTS_Z).astype(jnp.int32)
        factor_here = flat_blocks[positions]
        product_here = product[source_rows]
        partial_terms = jnp.einsum('tba,tybc->tyac', factor_here, product_here, precision=HIGHEST)
        selector = (product_cols[source_rows][:, :, None] == kept_row[None, None, :]).astype(jnp.float32)
        return jnp.einsum('tyx,tyac->xac', selector, partial_terms, precision=HIGHEST)

    metric = lax.map(metric_row, (jnp.arange(BLOCKS, dtype=jnp.int32), metric_cols))
    return product, metric
```

```python
import functools

import jax
import jax.numpy as jnp
from jax import lax
from jax.experimental import pallas as pl
from jax.experimental.pallas import tpu as pltpu
from jax.sharding import PartitionSpec as P

F32 = jnp.float32
BF16 = jnp.bfloat16
WINDOW = 36


def ring(array, by):
    devices = lax.axis_size("rows")
    return lax.ppermute(array, "rows", [(i, (i + by) % devices) for i in range(devices)])


def swap(array):
    return lax.ppermute(array, "rep", [(0, 1), (1, 0)])


def split(block):
    high = block.astype(BF16)
    return high, (block - high.astype(F32)).astype(BF16)


def wrap(index, total):
    if total & (total - 1) == 0:
        return jnp.bitwise_and(index, total - 1)
    return lax.rem(index + total, total)


def clear(ref, first=0, last=None):
    zero = jnp.zeros(ref.shape[1:], ref.dtype)

    def body(i, carry):
        ref[i] = zero
        return carry

    lax.fori_loop(first, ref.shape[0] if last is None else last, body, 0, unroll=4)


def margin_left_kernel(total, meta, cols_a, cols_b, table_a, table_b, out):
    position, core = meta[0], meta[1]
    for group in range(5):
        for c in range(2):
            clear(out.at[group, c])
    first = 4 * position - 8
    for cols, table in ((cols_a, table_a), (cols_b, table_b)):
        for row in range(4):

            def body(k, carry, cols=cols, table=table, row=row):
                rel = wrap(cols[row, k] - first, total)
                within = jnp.bitwise_and(rel, 3) - 2 * core

                @pl.when((within >= 0) & (within < 2))
                def _():
                    group = lax.shift_right_logical(rel, 2)
                    high, low = split(table[row, k])
                    out[group, within, row, :, :128] = high
                    out[group, within, row, :, 128:] = low

                return carry

            lax.fori_loop(0, table.shape[1], body, 0)


def factor_left_kernel(total, meta, *refs):
    patterns, tables, out = refs[:5], refs[5:15], refs[15]
    position = meta[0]
    for group in range(5):
        for c in range(2):
            clear(out.at[group, c])
            cols, table = patterns[group], tables[2 * group + c]

            def body(m, carry, cols=cols, table=table, group=group, c=c):
                rel = wrap(cols[c, m] - 4 * position, total)

                @pl.when(rel < 4)
                def _():
                    high, low = split(table[m].T)
                    out[group, c, rel, :, :128] = high
                    out[group, c, rel, :, 128:] = low

                return carry

            lax.fori_loop(0, table.shape[0], body, 0)


def stage_kernel(gs, crs, starts, counts, total, by_rows, row0, col0, has_acc, *refs):
    count, depth = len(gs), len(crs)
    meta, outcols = refs[:2]
    patterns = refs[2 : 2 + count]
    refs = refs[2 + count :]
    lefts, tables = refs[0], refs[1 : 1 + count * depth]
    refs = refs[1 + count * depth :]
    acc = None
    if has_acc:
        acc, refs = refs[:2], refs[2:]
    outs, refs = refs[:2], refs[2:]
    right_high, right_low, dense = refs
    core = meta[1]
    base = 4 * meta[0] - 16
    rows = dense.shape[1]
    spare = right_high.shape[1] - 1
    for gi in range(count):
        clear(right_high.at[gi], 0, counts[gi])
        clear(right_low.at[gi], 0, counts[gi])
        for ci, c in enumerate(crs):
            cols, table = patterns[gi], tables[gi * depth + ci]

            def right_body(m, carry, gi=gi, ci=ci, c=c, cols=cols, table=table):
                rel = wrap(cols[c, col0 + m] - base, total) - starts[gi]
                rel = jnp.where((rel >= 0) & (rel < counts[gi]), rel, spare)
                high, low = split(table[m])
                right_high[gi, rel, ci] = high
                right_low[gi, rel, ci] = low
                return carry

            lax.fori_loop(0, table.shape[0], right_body, 0, unroll=4)

    def left_of(g, c):
        if rows == 4:
            return lefts[g + 2, c]
        if by_rows:
            return jnp.stack([lefts[g + 2, c, row0], lefts[g + 2, c, 2 + row0]])
        return lefts[g + 2, c, row0 : row0 + 2]

    def rights(ref, gi, at):
        return jnp.concatenate(
            [ref[gi, at].reshape(128 * depth, 128), ref[gi, at + 1].reshape(128 * depth, 128)], axis=1
        )

    done = (0, 0)
    for gi, g in enumerate(gs):
        left = [left_of(g, c).reshape(rows * 128, 256) for c in crs]
        highs = [part[:, :128] for part in left]
        lows = [part[:, 128:] for part in left]
        left = jnp.concatenate(highs + lows + highs, axis=1)

        def body(q, carry, gi=gi, left=left, add=False):
            rh, rl = rights(right_high, gi, 2 * q), rights(right_low, gi, 2 * q)
            out = jnp.dot(left, jnp.concatenate([rh, rh, rl], axis=0), preferred_element_type=F32)
            to = starts[gi] + 2 * q
            for j in range(2):
                value = out[:, 128 * j : 128 * j + 128].reshape(rows, 128, 128)
                dense[to + j] = dense[to + j] + value if add else value
            return carry

        start, stop = starts[gi], starts[gi] + counts[gi]
        low, high = max(start, done[0]), min(stop, done[1])
        if low >= high:
            spans = [(start, stop, False)]
        else:
            spans = [(start, low, False), (low, high, True), (high, stop, False)]
        for first, last, add in spans:
            if last > first:
                lax.fori_loop(
                    (first - start) // 2, (last - start) // 2, functools.partial(body, add=add), 0, unroll=2
                )
        done = (start, stop) if gi == 0 else (min(start, done[0]), max(stop, done[1]))
    clear(dense, 0, done[0])
    clear(dense, done[1], WINDOW)
    kept_rows, kept_cols = outs[0].shape[:2]
    for which in range(2):
        side = core if which == 0 else 1 - core
        for row in range(kept_rows):
            source = side * kept_rows + row if by_rows else row
            at_row = 2 * side + row0 + row if by_rows else row0 + row
            at_col = 0 if by_rows else kept_cols * side

            def out_body(y, carry, which=which, row=row, source=source, at_row=at_row, at_col=at_col):
                rel = wrap(outcols[at_row, at_col + y] - base, total)
                value = dense[rel, source]
                if acc is not None:
                    value = value + acc[which][row, y]
                outs[which][row, y] = value
                return carry

            lax.fori_loop(0, kept_cols, out_body, 0, unroll=4)


SMEM = pl.BlockSpec(memory_space=pltpu.SMEM)
VMEM = pl.BlockSpec(memory_space=pltpu.VMEM)
PARAMS = pltpu.CompilerParams(vmem_limit_bytes=60 << 20)


def stage(name, gs, crs, by_rows, part, total, meta, outcols, patterns, left, tables, acc, col0):
    if by_rows:
        starts, counts = [4 * (g + 2) for g in gs], [20] * len(gs)
        out = (2 if part is None else 1, outcols.shape[1], 128, 128)
        row0, rows = part or 0, 2 * out[0]
    else:
        starts, counts = [max(0, 4 * g) for g in gs], [WINDOW - 4 * abs(g) for g in gs]
        out = (4 if part is None else 2, outcols.shape[1] // 2, 128, 128)
        row0, rows = 2 * (part or 0), out[0]
    kernel = functools.partial(
        stage_kernel, gs, crs, starts, counts, total, by_rows, row0, col0, bool(acc)
    )
    shape = jax.ShapeDtypeStruct(out, F32)
    blocks = [tables[g][c] for g in gs for c in crs]
    window = max(counts)
    return pl.pallas_call(
        kernel,
        name=name,
        out_shape=[shape, shape],
        in_specs=[SMEM] * (2 + len(gs)) + [VMEM] * (1 + len(blocks) + len(acc)),
        out_specs=[VMEM, VMEM],
        scratch_shapes=[
            pltpu.VMEM((len(gs), window + 1, len(crs), 128, 128), BF16),
            pltpu.VMEM((len(gs), window + 1, len(crs), 128, 128), BF16),
            pltpu.VMEM((WINDOW, rows, 128, 128), F32),
        ],
        compiler_params=PARAMS,
        cost_estimate=pl.CostEstimate(
            flops=0,
            transcendentals=0,
            bytes_accessed=0,
        ),
    )(meta, outcols, *[patterns[g] for g in gs], left, *blocks, *acc)


def left_call(kernel, name, scalars, arrays):
    out = jax.ShapeDtypeStruct((5, 2, 4, 128, 256), BF16)
    return pl.pallas_call(
        kernel,
        name=name,
        out_shape=out,
        in_specs=[SMEM] * len(scalars) + [VMEM] * len(arrays),
        out_specs=VMEM,
        compiler_params=PARAMS,
        cost_estimate=pl.CostEstimate(
            flops=0, transcendentals=0, bytes_accessed=0
        ),
    )(*scalars, *arrays)


def halo(own, after_near):
    tables = {0: own}
    near = {g: [ring(a, -g) for a in own] for g in (-1, 1)}
    tables.update(near)
    (first, second), tied = after_near((near[-1][0], near[1][0]))
    tables[-2] = [ring(first, 1)]
    tables[2] = [ring(second, -1)]
    tables[-2].append(ring(near[-1][1], 1))
    tables[2].append(ring(near[1][1], -1))
    return tables, tied


def shards(margin_blocks, margin_cols, factor_blocks, factor_cols, product_cols, metric_cols):
    total = factor_blocks.shape[0] * lax.axis_size("rows")
    position = lax.axis_index("rows")
    core = lax.axis_index("rep")
    meta = jnp.stack([position, core]).astype(jnp.int32)
    slots = factor_cols.shape[1]
    own = [lax.dynamic_index_in_dim(factor_blocks, 2 * core + c, 0, keepdims=False) for c in range(2)]
    patterns = {0: lax.dynamic_slice_in_dim(jnp.concatenate([factor_cols, product_cols], axis=1), 2 * core, 2, 0)}
    for g in (-2, -1, 1, 2):
        patterns[g] = ring(patterns[0], -g)

    def margin_after(near):
        other = swap(margin_blocks)
        other_cols = swap(margin_cols)
        left = left_call(
            functools.partial(margin_left_kernel, total), "margin_left",
            [meta, margin_cols, other_cols], [margin_blocks, other],
        )
        return lax.optimization_barrier((near, (left, patterns)))

    factors, (left, patterns) = halo(own, margin_after)
    part = lambda name, gs, crs, which, acc: stage(
        name, gs, crs, True, which, total, meta, product_cols, patterns, left, factors, acc, 0
    )
    acc = part("product_near", (0, -1, 1), (0, 1), None, ())
    acc = part("product_far0", (-2, 2), (0,), None, acc)
    base = acc[0] + swap(acc[1])
    finals = [part("product_far1", (-2, 2), (1,), which, ()) for which in range(2)]
    rows = [kept[0] + swap(sent)[0] + base[c] for c, (kept, sent) in enumerate(finals)]

    def product_after(near):
        both = jnp.stack(rows)
        width = both.shape[1] // 2
        mine = lax.dynamic_slice_in_dim(both, core * width, width, 1)
        theirs = swap(lax.dynamic_slice_in_dim(both, (1 - core) * width, width, 1))
        low, high = jnp.where(core == 0, mine, theirs), jnp.where(core == 0, theirs, mine)
        return lax.optimization_barrier((near, jnp.concatenate([low, high], axis=0)))

    products, product = halo(rows, product_after)
    left = left_call(
        functools.partial(factor_left_kernel, total), "factor_left",
        [meta] + [patterns[g] for g in range(-2, 3)], [factors[g][c] for g in range(-2, 3) for c in range(2)],
    )
    part = lambda name, gs, crs, which, acc: stage(
        name, gs, crs, False, which, total, meta, metric_cols, patterns, left, products, acc, slots
    )
    acc = part("metric_own", (0,), (0, 1), None, ())
    acc = part("metric_near", (-1, 1), (0, 1), None, acc)
    acc = part("metric_far0", (-2, 2), (0,), None, acc)
    base = acc[0] + swap(acc[1])
    finals = [part("metric_far1", (-2, 2), (1,), which, ()) for which in range(2)]
    metric = jnp.concatenate([kept + swap(sent) for kept, sent in finals], axis=0) + base
    return (product, metric)


def solution(mesh):
    return jax.shard_map(
        shards,
        mesh=mesh,
        in_specs=(
            P("rows", "rep", None, None),
            P("rows", "rep"),
            P("rows", None, None, None),
            P("rows", None),
            P("rows", None),
            P("rows", None),
        ),
        out_specs=(P("rows", "rep", None, None), P("rows", "rep", None, None)),
        check_vma=False,
    )
```

```python
import functools

import jax
import jax.numpy as jnp
from jax import lax
from jax.experimental import pallas as pl
from jax.experimental.pallas import tpu as pltpu
from jax.sharding import PartitionSpec as P

F32 = jnp.float32
BF16 = jnp.bfloat16
WINDOW = 36


def ring(array, by):
    devices = lax.axis_size("rows")
    return lax.ppermute(array, "rows", [(i, (i + by) % devices) for i in range(devices)])


def swap(array):
    return lax.ppermute(array, "rep", [(0, 1), (1, 0)])


def split(block):
    high = block.astype(BF16)
    return high, (block - high.astype(F32)).astype(BF16)


def block_of(table, index):
    return table[pl.ds(pl.multiple_of(index * 128, 128), 128), :]


def wrap(index, total):
    if total & (total - 1) == 0:
        return jnp.bitwise_and(index, total - 1)
    return lax.rem(index + total, total)


def clear(ref, first=0, last=None):
    zero = jnp.zeros(ref.shape[1:], ref.dtype)

    def body(i, carry):
        ref[i] = zero
        return carry

    lax.fori_loop(first, ref.shape[0] if last is None else last, body, 0, unroll=4)


def copy_last(out, parts, row_of):
    for part, ref in enumerate(parts):
        for gi, group in enumerate((0, 4)):
            for row in range(2):
                ref[gi, 0, row] = out[group, 1, row_of(part, row)]


def margin_left_kernel(total, meta, cols_a, cols_b, table_a, table_b, out, part_a, part_b):
    position, core = meta[0], meta[1]
    for group in range(5):
        for c in range(2):
            clear(out.at[group, c])
    first = 4 * position - 8
    for cols, table in ((cols_a, table_a), (cols_b, table_b)):
        for row in range(4):

            def body(k, carry, cols=cols, table=table, row=row):
                rel = wrap(cols[row, k] - first, total)
                within = jnp.bitwise_and(rel, 3) - 2 * core

                @pl.when((within >= 0) & (within < 2))
                def _():
                    group = lax.shift_right_logical(rel, 2)
                    high, low = split(table[row, k])
                    out[group, within, row, :, :128] = high
                    out[group, within, row, :, 128:] = low

                return carry

            lax.fori_loop(0, table.shape[1], body, 0)
    copy_last(out, (part_a, part_b), lambda part, row: 2 * row + part)


def factor_left_kernel(pieces, total, meta, *refs):
    patterns, refs = refs[:5], refs[5:]
    out, part_a, part_b = refs[-3:]
    tables, refs = [], list(refs[:-3])
    for number in pieces:
        tables.append([refs.pop(0) for _ in range(number)])
    position = meta[0]
    for group in range(5):
        for c in range(2):
            clear(out.at[group, c])
            cols, first = patterns[group], 0
            for table in tables[2 * group + c]:

                def body(m, carry, cols=cols, table=table, group=group, c=c, first=first):
                    rel = wrap(cols[c, first + m] - 4 * position, total)

                    @pl.when(rel < 4)
                    def _():
                        high, low = split(block_of(table, m).T)
                        out[group, c, rel, :, :128] = high
                        out[group, c, rel, :, 128:] = low

                    return carry

                lax.fori_loop(0, table.shape[0] // 128, body, 0)
                first += table.shape[0] // 128
    copy_last(out, (part_a, part_b), lambda part, row: 2 * part + row)


def stage_kernel(gs, crs, pieces, starts, counts, total, by_rows, row0, col0, has_acc, *refs):
    count, depth = len(gs), len(crs)
    meta, outcols = refs[:2]
    patterns = refs[2 : 2 + count]
    refs = refs[2 + count :]
    lefts, refs = refs[0], list(refs[1:])
    tables = []
    for number in pieces:
        tables.append([refs.pop(0) for _ in range(number)])
    acc = None
    if has_acc:
        acc, refs = refs[:2], refs[2:]
    right_high, right_low, dense = refs[-3:]
    outs = refs[:-3]
    portions = len(outs) // 2
    core = meta[1]
    base = 4 * meta[0] - 16
    rows = dense.shape[1]
    spare = right_high.shape[1] - 1
    for gi in range(count):
        clear(right_high.at[gi], 0, counts[gi])
        clear(right_low.at[gi], 0, counts[gi])
        for ci, c in enumerate(crs):
            cols, first = patterns[gi], col0
            for table in tables[gi * depth + ci]:

                def right_body(m, carry, gi=gi, ci=ci, c=c, cols=cols, table=table, first=first):
                    rel = wrap(cols[c, first + m] - base, total) - starts[gi]
                    rel = jnp.where((rel >= 0) & (rel < counts[gi]), rel, spare)
                    high, low = split(block_of(table, m))
                    right_high[gi, rel, ci] = high
                    right_low[gi, rel, ci] = low
                    return carry

                lax.fori_loop(0, table.shape[0] // 128, right_body, 0, unroll=4)
                first += table.shape[0] // 128

    def rights(ref, gi, at):
        return jnp.concatenate(
            [ref[gi, at + j].reshape(128 * depth, 128) for j in range(4)], axis=1
        )

    done = (0, 0)
    for gi, g in enumerate(gs):
        if lefts.shape[0] == 5:
            left = [lefts[g + 2, c].reshape(rows * 128, 256) for c in crs]
        else:
            left = [lefts[gi, 0].reshape(rows * 128, 256)]
        highs = [part[:, :128] for part in left]
        lows = [part[:, 128:] for part in left]
        left = jnp.concatenate(highs + lows + highs, axis=1)

        def body(q, carry, gi=gi, left=left, add=False):
            rh, rl = rights(right_high, gi, 4 * q), rights(right_low, gi, 4 * q)
            out = jnp.dot(left, jnp.concatenate([rh, rh, rl], axis=0), preferred_element_type=F32)
            to = starts[gi] + 4 * q
            for j in range(4):
                value = out[:, 128 * j : 128 * j + 128].reshape(rows, 128, 128)
                dense[to + j] = dense[to + j] + value if add else value
            return carry

        start, stop = starts[gi], starts[gi] + counts[gi]
        low, high = max(start, done[0]), min(stop, done[1])
        if low >= high:
            spans = [(start, stop, False)]
        else:
            spans = [(start, low, False), (low, high, True), (high, stop, False)]
        for first, last, add in spans:
            if last > first:
                lax.fori_loop(
                    (first - start) // 4, (last - start) // 4, functools.partial(body, add=add), 0, unroll=2
                )
        done = (start, stop) if gi == 0 else (min(start, done[0]), max(stop, done[1]))
    clear(dense, 0, done[0])
    clear(dense, done[1], WINDOW)
    kept_rows, kept_cols = outs[0].shape[0] * portions, outs[0].shape[1]
    each = outs[0].shape[0]
    for which in range(2):
        side = core if which == 0 else 1 - core
        for row in range(kept_rows):
            source = side * kept_rows + row if by_rows else row
            at_row = 2 * side + row0 + row if by_rows else row0 + row
            at_col = 0 if by_rows else kept_cols * side

            def out_body(y, carry, which=which, row=row, source=source, at_row=at_row, at_col=at_col):
                rel = wrap(outcols[at_row, at_col + y] - base, total)
                value = dense[rel, source]
                if acc is not None:
                    value = value + acc[which][row, y]
                outs[which * portions + row // each][row % each, y] = value
                return carry

            lax.fori_loop(0, kept_cols, out_body, 0, unroll=4)


SMEM = pl.BlockSpec(memory_space=pltpu.SMEM)
VMEM = pl.BlockSpec(memory_space=pltpu.VMEM)
PARAMS = pltpu.CompilerParams(vmem_limit_bytes=60 << 20)


def stage(name, gs, crs, by_rows, part, total, meta, outcols, patterns, left, tables, acc, col0, portions=1):
    if by_rows:
        starts, counts = [4 * (g + 2) for g in gs], [20] * len(gs)
        out = (2 if part is None else 1, outcols.shape[1], 128, 128)
        row0, rows = part or 0, 2 * out[0]
    else:
        starts, counts = [max(0, 4 * g) for g in gs], [WINDOW - 4 * abs(g) for g in gs]
        out = (4 if part is None else 2, outcols.shape[1] // 2, 128, 128)
        row0, rows = 2 * (part or 0), out[0]
    tables = [tables[g][c] for g in gs for c in crs]
    kernel = functools.partial(
        stage_kernel, gs, crs, [len(t) for t in tables], starts, counts, total, by_rows, row0, col0, bool(acc)
    )
    shape = jax.ShapeDtypeStruct((out[0] // portions,) + out[1:], F32)
    blocks = [piece for table in tables for piece in table]
    window = max(counts)
    return pl.pallas_call(
        kernel,
        name=name,
        out_shape=[shape] * (2 * portions),
        in_specs=[SMEM] * (2 + len(gs)) + [VMEM] * (1 + len(blocks) + len(acc)),
        out_specs=[VMEM] * (2 * portions),
        scratch_shapes=[
            pltpu.VMEM((len(gs), window + 1, len(crs), 128, 128), BF16),
            pltpu.VMEM((len(gs), window + 1, len(crs), 128, 128), BF16),
            pltpu.VMEM((WINDOW, rows, 128, 128), F32),
        ],
        compiler_params=PARAMS,
        cost_estimate=pl.CostEstimate(
            flops=0,
            transcendentals=0,
            bytes_accessed=0,
        ),
    )(
        meta, outcols, *[patterns[g] for g in gs], left[0 if part is None else 1 + part], *blocks, *acc
    )


def left_call(kernel, name, scalars, arrays):
    out = jax.ShapeDtypeStruct((5, 2, 4, 128, 256), BF16)
    last = jax.ShapeDtypeStruct((2, 1, 2, 128, 256), BF16)
    return pl.pallas_call(
        kernel,
        name=name,
        out_shape=[out, last, last],
        in_specs=[SMEM] * len(scalars) + [VMEM] * len(arrays),
        out_specs=[VMEM] * 3,
        compiler_params=PARAMS,
        cost_estimate=pl.CostEstimate(
            flops=0, transcendentals=0, bytes_accessed=0
        ),
    )(*scalars, *arrays)


def halo(own, after_first, before_last):
    first, last = ({g: ring(row, -g) for g in (-1, 1)} for row in own)
    near = after_first(first[-1], first[1])
    first[-2], first[2] = ring(near[0], 1), ring(near[1], -1)
    near = before_last(last[-1], last[1])
    last[-2], last[2] = ring(near[0], 1), ring(near[1], -1)
    tables = {g: [(first[g],), (last[g],)] for g in (-2, -1, 1, 2)}
    tables[0] = [(row,) for row in own]
    return tables


def shards(margin_blocks, margin_cols, factor_blocks, factor_cols, product_cols, metric_cols):
    total = factor_blocks.shape[0] * lax.axis_size("rows")
    position = lax.axis_index("rows")
    core = lax.axis_index("rep")
    meta = jnp.stack([position, core]).astype(jnp.int32)
    slots = factor_cols.shape[1]
    pattern = lax.dynamic_slice_in_dim(jnp.concatenate([factor_cols, product_cols], axis=1), 2 * core, 2, 0)
    own = [
        lax.dynamic_index_in_dim(factor_blocks, 2 * core + c, 0, keepdims=False).reshape(slots * 128, 128)
        for c in range(2)
    ]
    columns = jnp.pad(pattern.astype(F32), ((0, 6), (0, 128 - pattern.shape[1])))
    own[0] = jnp.concatenate([own[0], columns], axis=0)
    margin_left = left_call(
        functools.partial(margin_left_kernel, total), "margin_left",
        [meta, margin_cols, swap(margin_cols)], [margin_blocks, swap(margin_blocks)],
    )

    def after_margin(below, above):
        return lax.optimization_barrier((below, above, margin_left))[:2]

    factors = halo(own, after_margin, lambda below, above: (below, above))
    patterns = {0: pattern}
    for g in (-2, -1, 1, 2):
        patterns[g] = factors[g][0][0][slots * 128 : slots * 128 + 2, : pattern.shape[1]].astype(jnp.int32)
    part = lambda name, gs, crs, which, acc: stage(
        name, gs, crs, True, which, total, meta, product_cols, patterns, margin_left, factors, acc, 0,
        2 if gs == (-2, 2) and which is None else 1,
    )
    acc = part("product_near", (0, -1, 1), (0, 1), None, ())
    acc = part("product_far0", (-2, 2), (0,), None, acc)
    finals = [part("product_far1", (-2, 2), (1,), which, acc[which::2]) for which in range(2)]
    rows = [(kept + swap(sent))[0] for kept, sent in finals]
    both = jnp.stack(rows)
    rows = [row.reshape(-1, 128) for row in rows]
    half = both.shape[1] // 2
    mine = lax.dynamic_slice_in_dim(both, core * half, half, 1)
    theirs = swap(lax.dynamic_slice_in_dim(both, (1 - core) * half, half, 1))
    low, high = jnp.where(core == 0, mine, theirs), jnp.where(core == 0, theirs, mine)
    made = [jnp.concatenate([low, high], axis=0)]
    blocks = [factors[g][c] for g in range(-2, 3) for c in range(2)]
    factor_left = left_call(
        functools.partial(factor_left_kernel, [len(b) for b in blocks], total), "factor_left",
        [meta] + [patterns[g] for g in range(-2, 3)], [piece for b in blocks for piece in b],
    )
    products = {0: [(row,) for row in rows]}
    part = lambda name, gs, crs, which, acc: stage(
        name, gs, crs, False, which, total, meta, metric_cols, patterns, factor_left, products, acc, slots,
        2 if gs == (-2, 2) and which is None else 1,
    )
    own_acc = part("metric_own", (0,), (0, 1), None, ())

    def after_own(below, above):
        return lax.optimization_barrier((below, above, tuple(own_acc)))[:2]

    def finish_product(below, above):
        below, above, made[0] = lax.optimization_barrier((below, above, made[0]))
        return below, above

    products = halo(rows, after_own, finish_product)
    acc = part("metric_near", (-1, 1), (0, 1), None, own_acc)
    acc = part("metric_far0", (-2, 2), (0,), None, acc)
    finals = [part("metric_far1", (-2, 2), (1,), which, acc[which::2]) for which in range(2)]
    metric = jnp.concatenate([kept + swap(sent) for kept, sent in finals], axis=0)
    return (made[0], metric)


def solution(mesh):
    return jax.shard_map(
        shards,
        mesh=mesh,
        in_specs=(
            P("rows", "rep", None, None),
            P("rows", "rep"),
            P("rows", None, None, None),
            P("rows", None),
            P("rows", None),
            P("rows", None),
        ),
        out_specs=(P("rows", "rep", None, None), P("rows", "rep", None, None)),
        check_vma=False,
    )
```

```python
import functools

import jax
import jax.numpy as jnp
from jax import lax
from jax.experimental import pallas as pl
from jax.experimental.pallas import tpu as pltpu
from jax.sharding import PartitionSpec as P

F32 = jnp.float32
BF16 = jnp.bfloat16
WINDOW = 36


def ring(array, by):
    devices = lax.axis_size("rows")
    return lax.ppermute(array, "rows", [(i, (i + by) % devices) for i in range(devices)])


def swap(array):
    return lax.ppermute(array, "rep", [(0, 1), (1, 0)])


def split(block):
    high = block.astype(BF16)
    return high, (block - high.astype(F32)).astype(BF16)


def block_of(table, index):
    return table[pl.ds(pl.multiple_of(index * 128, 128), 128), :]


def wrap(index, total):
    if total & (total - 1) == 0:
        return jnp.bitwise_and(index, total - 1)
    return lax.rem(index + total, total)


def clear(ref, first=0, last=None):
    zero = jnp.zeros(ref.shape[1:], ref.dtype)

    def body(i, carry):
        ref[i] = zero
        return carry

    lax.fori_loop(first, ref.shape[0] if last is None else last, body, 0, unroll=4)


def copy_last(out, parts, row_of):
    for part, ref in enumerate(parts):
        for gi, group in enumerate((0, 4)):
            for row in range(2):
                ref[gi, 0, row] = out[group, 1, row_of(part, row)]


def margin_left_kernel(total, meta, cols_a, cols_b, table_a, table_b, out, part_a, part_b):
    position, core = meta[0], meta[1]
    for group in range(5):
        for c in range(2):
            clear(out.at[group, c])
    first = 4 * position - 8
    for cols, table in ((cols_a, table_a), (cols_b, table_b)):
        for row in range(4):

            def body(k, carry, cols=cols, table=table, row=row):
                rel = wrap(cols[row, k] - first, total)
                within = jnp.bitwise_and(rel, 3) - 2 * core

                @pl.when((within >= 0) & (within < 2))
                def _():
                    group = lax.shift_right_logical(rel, 2)
                    high, low = split(table[row, k])
                    out[group, within, row, :, :128] = high
                    out[group, within, row, :, 128:] = low

                return carry

            lax.fori_loop(0, table.shape[1], body, 0)
    copy_last(out, (part_a, part_b), lambda part, row: 2 * row + part)


def factor_left_kernel(pieces, total, meta, *refs):
    patterns, refs = refs[:5], refs[5:]
    out, part_a, part_b = refs[-3:]
    tables, refs = [], list(refs[:-3])
    for number in pieces:
        tables.append([refs.pop(0) for _ in range(number)])
    position = meta[0]
    for group in range(5):
        for c in range(2):
            clear(out.at[group, c])
            cols, first = patterns[group], 0
            for table in tables[2 * group + c]:

                def body(m, carry, cols=cols, table=table, group=group, c=c, first=first):
                    rel = wrap(cols[c, first + m] - 4 * position, total)

                    @pl.when(rel < 4)
                    def _():
                        high, low = split(block_of(table, m).T)
                        out[group, c, rel, :, :128] = high
                        out[group, c, rel, :, 128:] = low

                    return carry

                lax.fori_loop(0, table.shape[0] // 128, body, 0)
                first += table.shape[0] // 128
    copy_last(out, (part_a, part_b), lambda part, row: 2 * part + row)


def stage_kernel(gs, crs, pieces, starts, counts, total, by_rows, row0, col0, has_acc, portions, *refs):
    count, depth = len(gs), len(crs)
    meta, outcols = refs[:2]
    patterns = refs[2 : 2 + count]
    refs = refs[2 + count :]
    lefts, refs = refs[0], list(refs[1:])
    sources = [refs.pop(0) for _ in range(sum(pieces))]
    acc_sources = [refs.pop(0) for _ in range(2 if has_acc else 0)]
    results = [refs.pop(0) for _ in range(2 * portions)]
    right_high, right_low, dense, left_held, sems = refs[:5]
    refs = refs[5:]
    held = [refs.pop(0) for _ in sources]
    acc = [refs.pop(0) for _ in acc_sources]
    outs = refs
    copies = []

    def start(source, target):
        copies.append(pltpu.make_async_copy(source, target, sems.at[len(copies)]))
        copies[-1].start()
        return copies[-1]

    arriving = [start(source.at[pl.ds(0, target.shape[0])], target) for source, target in zip(sources, held)]
    left_copies = []
    for gi, g in enumerate(gs):
        for ci, c in enumerate(crs):
            source = lefts.at[g + 2, c] if lefts.shape[0] == 5 else lefts.at[gi, 0]
            left_copies.append(start(source, left_held.at[gi, ci]))
    acc_copies = [start(source, target) for source, target in zip(acc_sources, acc)]
    tables, held = [], list(zip(held, arriving))
    for number in pieces:
        tables.append([held.pop(0) for _ in range(number)])
    core = meta[1]
    base = 4 * meta[0] - 16
    rows = dense.shape[1]
    spare = right_high.shape[1] - 1
    for gi in range(count):
        clear(right_high.at[gi], 0, counts[gi])
        clear(right_low.at[gi], 0, counts[gi])
    for gi in range(count):
        for ci, c in enumerate(crs):
            cols, first = patterns[gi], col0
            for table, copy in tables[gi * depth + ci]:
                copy.wait()

                def right_body(m, carry, gi=gi, ci=ci, c=c, cols=cols, table=table, first=first):
                    rel = wrap(cols[c, first + m] - base, total) - starts[gi]
                    rel = jnp.where((rel >= 0) & (rel < counts[gi]), rel, spare)
                    high, low = split(block_of(table, m))
                    right_high[gi, rel, ci] = high
                    right_low[gi, rel, ci] = low
                    return carry

                lax.fori_loop(0, table.shape[0] // 128, right_body, 0, unroll=4)
                first += table.shape[0] // 128

    def rights(ref, gi, at):
        return jnp.concatenate(
            [ref[gi, at + j].reshape(128 * depth, 128) for j in range(4)], axis=1
        )

    for copy in left_copies:
        copy.wait()
    lefts_of = []
    for gi in range(count):
        left = [left_held[gi, ci].reshape(rows * 128, 256) for ci in range(depth)]
        highs = [part[:, :128] for part in left]
        lows = [part[:, 128:] for part in left]
        lefts_of.append(highs + lows + highs)

    edges = sorted({0, WINDOW} | set(starts) | {s + c for s, c in zip(starts, counts)})
    for first, last in zip(edges, edges[1:]):
        active = [gi for gi in range(count) if starts[gi] <= first and last <= starts[gi] + counts[gi]]
        if not active:
            clear(dense, first, last)
            continue
        left = jnp.concatenate([part for gi in active for part in lefts_of[gi]], axis=1)

        def body(q, carry, active=active, left=left):
            right = []
            for gi in active:
                rh = rights(right_high, gi, 4 * q - starts[gi])
                right += [rh, rh, rights(right_low, gi, 4 * q - starts[gi])]
            out = jnp.dot(left, jnp.concatenate(right, axis=0), preferred_element_type=F32)
            for j in range(4):
                dense[4 * q + j] = out[:, 128 * j : 128 * j + 128].reshape(rows, 128, 128)
            return carry

        lax.fori_loop(first // 4, last // 4, body, 0, unroll=2)
    for copy in acc_copies:
        copy.wait()
    each, kept_cols = outs[0].shape[:2]
    leaving = []
    for which in (1, 0):
        side = core if which == 0 else 1 - core
        for row in range(each * portions):
            source = side * each * portions + row if by_rows else row
            at_row = 2 * side + row0 + row if by_rows else row0 + row
            at_col = 0 if by_rows else kept_cols * side
            portion = which * portions + row // each
            own, sum_in = outs[portion].at[row % each], acc[which].at[row] if acc else None

            def out_body(y, carry, own=own, sum_in=sum_in, source=source, at_row=at_row, at_col=at_col):
                value = dense[wrap(outcols[at_row, at_col + y] - base, total), source]
                own[y] = value if sum_in is None else value + sum_in[y]
                return carry

            lax.fori_loop(0, kept_cols, out_body, 0, unroll=4)
            leaving.append(start(own, results[portion].at[row % each]))
    for copy in leaving:
        copy.wait()


SMEM = pl.BlockSpec(memory_space=pltpu.SMEM)
VMEM = pl.BlockSpec(memory_space=pltpu.VMEM)
HERE = pl.BlockSpec(memory_space=pl.ANY)
PARAMS = pltpu.CompilerParams(vmem_limit_bytes=60 << 20)


def stage(name, gs, crs, by_rows, part, total, meta, outcols, patterns, left, tables, acc, col0, portions=1):
    if by_rows:
        starts, counts = [4 * (g + 2) for g in gs], [20] * len(gs)
        out = (2 if part is None else 1, outcols.shape[1], 128, 128)
        row0, rows = part or 0, 2 * out[0]
    else:
        starts, counts = [max(0, 4 * g) for g in gs], [WINDOW - 4 * abs(g) for g in gs]
        out = (4 if part is None else 2, outcols.shape[1] // 2, 128, 128)
        row0, rows = 2 * (part or 0), out[0]
    tables = [tables[g][c] for g in gs for c in crs]
    kernel = functools.partial(
        stage_kernel, gs, crs, [len(t) for t in tables], starts, counts, total, by_rows, row0, col0, bool(acc), portions
    )
    shape = jax.ShapeDtypeStruct((out[0] // portions,) + out[1:], F32)
    blocks = [piece for table in tables for piece in table]
    window = max(counts)
    return pl.pallas_call(
        kernel,
        name=name,
        out_shape=[shape] * (2 * portions),
        in_specs=[SMEM] * (2 + len(gs)) + [HERE] * (1 + len(blocks) + len(acc)),
        out_specs=[HERE] * (2 * portions),
        scratch_shapes=[
            pltpu.VMEM((len(gs), window + 1, len(crs), 128, 128), BF16),
            pltpu.VMEM((len(gs), window + 1, len(crs), 128, 128), BF16),
            pltpu.VMEM((WINDOW, rows, 128, 128), F32),
            pltpu.VMEM((len(gs), len(crs), rows, 128, 256), BF16),
            pltpu.SemaphoreType.DMA((len(blocks) + len(gs) * len(crs) + len(acc) + 2 * out[0],)),
        ]
        + [pltpu.VMEM((b.shape[0] // 128 * 128, 128), F32) for b in blocks]
        + [pltpu.VMEM(a.shape, F32) for a in acc]
        + [pltpu.VMEM(shape.shape, F32)] * (2 * portions),
        compiler_params=PARAMS,
        cost_estimate=pl.CostEstimate(
            flops=0,
            transcendentals=0,
            bytes_accessed=0,
        ),
    )(
        meta, outcols, *[patterns[g] for g in gs], left[0 if part is None else 1 + part], *blocks, *acc
    )


def left_call(kernel, name, scalars, arrays):
    out = jax.ShapeDtypeStruct((5, 2, 4, 128, 256), BF16)
    last = jax.ShapeDtypeStruct((2, 1, 2, 128, 256), BF16)
    return pl.pallas_call(
        kernel,
        name=name,
        out_shape=[out, last, last],
        in_specs=[SMEM] * len(scalars) + [VMEM] * len(arrays),
        out_specs=[VMEM] * 3,
        compiler_params=PARAMS,
        cost_estimate=pl.CostEstimate(
            flops=0, transcendentals=0, bytes_accessed=0
        ),
    )(*scalars, *arrays)


def halo(own, after_first, before_last):
    first, last = ({g: ring(row, -g) for g in (-1, 1)} for row in own)
    near = after_first(first[-1], first[1])
    first[-2], first[2] = ring(near[0], 1), ring(near[1], -1)
    near = before_last(last[-1], last[1])
    last[-2], last[2] = ring(near[0], 1), ring(near[1], -1)
    tables = {g: [(first[g],), (last[g],)] for g in (-2, -1, 1, 2)}
    tables[0] = [(row,) for row in own]
    return tables


def shards(margin_blocks, margin_cols, factor_blocks, factor_cols, product_cols, metric_cols):
    total = factor_blocks.shape[0] * lax.axis_size("rows")
    position = lax.axis_index("rows")
    core = lax.axis_index("rep")
    meta = jnp.stack([position, core]).astype(jnp.int32)
    slots = factor_cols.shape[1]
    pattern = lax.dynamic_slice_in_dim(jnp.concatenate([factor_cols, product_cols], axis=1), 2 * core, 2, 0)
    own = [
        lax.dynamic_index_in_dim(factor_blocks, 2 * core + c, 0, keepdims=False).reshape(slots * 128, 128)
        for c in range(2)
    ]
    columns = jnp.pad(pattern.astype(F32), ((0, 6), (0, 128 - pattern.shape[1])))
    own[0] = jnp.concatenate([own[0], columns], axis=0)
    margin_left = left_call(
        functools.partial(margin_left_kernel, total), "margin_left",
        [meta, margin_cols, swap(margin_cols)], [margin_blocks, swap(margin_blocks)],
    )

    def after_margin(below, above):
        return lax.optimization_barrier((below, above, margin_left))[:2]

    factors = halo(own, after_margin, lambda below, above: (below, above))
    patterns = {0: pattern}
    for g in (-2, -1, 1, 2):
        patterns[g] = factors[g][0][0][slots * 128 : slots * 128 + 2, : pattern.shape[1]].astype(jnp.int32)
    part = lambda name, gs, crs, which, acc: stage(
        name, gs, crs, True, which, total, meta, product_cols, patterns, margin_left, factors, acc, 0,
        2 if gs == (-2, 2) and which is None else 1,
    )
    acc = part("product_near", (0, -1, 1), (0, 1), None, ())
    acc = part("product_far0", (-2, 2), (0,), None, acc)
    finals = [part("product_far1", (-2, 2), (1,), which, acc[which::2]) for which in range(2)]
    rows = [(kept + swap(sent))[0] for kept, sent in finals]
    both = jnp.stack(rows)
    rows = [row.reshape(-1, 128) for row in rows]
    half = both.shape[1] // 2
    mine = lax.dynamic_slice_in_dim(both, core * half, half, 1)
    theirs = swap(lax.dynamic_slice_in_dim(both, (1 - core) * half, half, 1))
    low, high = jnp.where(core == 0, mine, theirs), jnp.where(core == 0, theirs, mine)
    made = [jnp.concatenate([low, high], axis=0)]
    blocks = [factors[g][c] for g in range(-2, 3) for c in range(2)]
    factor_left = left_call(
        functools.partial(factor_left_kernel, [len(b) for b in blocks], total), "factor_left",
        [meta] + [patterns[g] for g in range(-2, 3)], [piece for b in blocks for piece in b],
    )
    products = {0: [(row,) for row in rows]}
    part = lambda name, gs, crs, which, acc: stage(
        name, gs, crs, False, which, total, meta, metric_cols, patterns, factor_left, products, acc, slots,
        2 if gs == (-2, 2) and which is None else 1,
    )
    own_acc = part("metric_own", (0,), (0, 1), None, ())

    def after_own(below, above):
        return lax.optimization_barrier((below, above, tuple(own_acc)))[:2]

    def finish_product(below, above):
        below, above, made[0] = lax.optimization_barrier((below, above, made[0]))
        return below, above

    products = halo(rows, after_own, finish_product)
    acc = part("metric_near", (-1, 1), (0, 1), None, own_acc)
    acc = part("metric_far0", (-2, 2), (0,), None, acc)
    finals = [part("metric_far1", (-2, 2), (1,), which, acc[which::2]) for which in range(2)]
    metric = jnp.concatenate([kept + swap(sent) for kept, sent in finals], axis=0)
    return (made[0], metric)


def solution(mesh):
    return jax.shard_map(
        shards,
        mesh=mesh,
        in_specs=(
            P("rows", "rep", None, None),
            P("rows", "rep"),
            P("rows", None, None, None),
            P("rows", None),
            P("rows", None),
            P("rows", None),
        ),
        out_specs=(P("rows", "rep", None, None), P("rows", "rep", None, None)),
        check_vma=False,
    )
```

```python
import functools
import math

import jax
import jax.numpy as jnp
from jax import lax
from jax.experimental import pallas as pl
from jax.experimental.pallas import tpu as pltpu
from jax.sharding import PartitionSpec as P

F32 = jnp.float32
BF16 = jnp.bfloat16
WINDOW = 36


def ring(array, by):
    devices = lax.axis_size("rows")
    return lax.ppermute(array, "rows", [(i, (i + by) % devices) for i in range(devices)])


def swap(array):
    return lax.ppermute(array, "rep", [(0, 1), (1, 0)])


def split(block):
    high = block.astype(BF16)
    return high, (block - high.astype(F32)).astype(BF16)


def block_of(table, index):
    return table[pl.ds(pl.multiple_of(index * 128, 128), 128), :]


def wrap(index, total):
    if total & (total - 1) == 0:
        return jnp.bitwise_and(index, total - 1)
    return lax.rem(index + total, total)


def clear(ref, first=0, last=None):
    zero = jnp.zeros(ref.shape[1:], ref.dtype)

    def body(i, carry):
        ref[i] = zero
        return carry

    lax.fori_loop(first, ref.shape[0] if last is None else last, body, 0, unroll=4)


def copy_last(out, parts, row_of):
    for part, ref in enumerate(parts):
        for gi, group in enumerate((0, 4)):
            for row in range(2):
                ref[gi, 0, row] = out[group, 1, row_of(part, row)]


def margin_left_kernel(total, meta, cols_a, cols_b, table_a, table_b, out, part_a, part_b):
    position, core = meta[0], meta[1]
    for group in range(5):
        for c in range(2):
            clear(out.at[group, c])
    first = 4 * position - 8
    for cols, table in ((cols_a, table_a), (cols_b, table_b)):
        for row in range(4):

            def body(k, carry, cols=cols, table=table, row=row):
                rel = wrap(cols[row, k] - first, total)
                within = jnp.bitwise_and(rel, 3) - 2 * core

                @pl.when((within >= 0) & (within < 2))
                def _():
                    group = lax.shift_right_logical(rel, 2)
                    high, low = split(table[row, k])
                    out[group, within, row, :, :128] = high
                    out[group, within, row, :, 128:] = low

                return carry

            lax.fori_loop(0, table.shape[1], body, 0)
    copy_last(out, (part_a, part_b), lambda part, row: 2 * row + part)


def factor_left_kernel(pieces, total, meta, *refs):
    patterns, refs = refs[:5], refs[5:]
    out, part_a, part_b = refs[-3:]
    tables, refs = [], list(refs[:-3])
    for number in pieces:
        tables.append([refs.pop(0) for _ in range(number)])
    position = meta[0]
    for group in range(5):
        for c in range(2):
            clear(out.at[group, c])
            cols, first = patterns[group], 0
            for table in tables[2 * group + c]:

                def body(m, carry, cols=cols, table=table, group=group, c=c, first=first):
                    rel = wrap(cols[c, first + m] - 4 * position, total)

                    @pl.when(rel < 4)
                    def _():
                        high, low = split(block_of(table, m).T)
                        out[group, c, rel, :, :128] = high
                        out[group, c, rel, :, 128:] = low

                    return carry

                lax.fori_loop(0, table.shape[0] // 128, body, 0)
                first += table.shape[0] // 128
    copy_last(out, (part_a, part_b), lambda part, row: 2 * part + row)


def stage_kernel(gs, crs, pieces, starts, counts, total, by_rows, row0, col0, has_acc, portions, *refs):
    count, depth = len(gs), len(crs)
    meta, outcols = refs[:2]
    patterns = refs[2 : 2 + count]
    refs = refs[2 + count :]
    lefts, refs = refs[0], list(refs[1:])
    direct = lefts.shape[0] != 5
    sources = [refs.pop(0) for _ in range(sum(pieces))]
    acc_sources = [refs.pop(0) for _ in range(2 if has_acc else 0)]
    results = [refs.pop(0) for _ in range(2 * portions)]
    straight = portions == 2 or direct
    right_high, right_low, dense, left_held, sems = refs[:5]
    refs = refs[5:]
    held = sources if direct else [refs.pop(0) for _ in sources]
    acc = acc_sources if direct else [refs.pop(0) for _ in acc_sources]
    outs = results if straight else refs
    copies = []

    def start(source, target):
        copies.append(pltpu.make_async_copy(source, target, sems.at[len(copies)]))
        copies[-1].start()
        return copies[-1]

    arriving = [None if direct else start(source.at[pl.ds(0, target.shape[0])], target) for source, target in zip(sources, held)]
    left_copies = []
    for gi, g in enumerate(gs):
        for ci, c in enumerate(crs):
            source = lefts.at[g + 2, c] if lefts.shape[0] == 5 else lefts.at[gi, 0]
            left_copies.append(start(source, left_held.at[gi, ci]))
    acc_copies = [] if direct else [start(source, target) for source, target in zip(acc_sources, acc)]
    tables, held = [], list(zip(held, arriving))
    for number in pieces:
        tables.append([held.pop(0) for _ in range(number)])
    core = meta[1]
    base = 4 * meta[0] - 16
    rows = dense.shape[1]
    spare = right_high.shape[1] - 1
    for gi in range(count):
        clear(right_high.at[gi], 0, counts[gi])
        clear(right_low.at[gi], 0, counts[gi])
    for gi in range(count):
        for ci, c in enumerate(crs):
            cols, first = patterns[gi], col0
            for table, copy in tables[gi * depth + ci]:
                if copy is not None:
                    copy.wait()

                def right_body(m, carry, gi=gi, ci=ci, c=c, cols=cols, table=table, first=first):
                    rel = wrap(cols[c, first + m] - base, total) - starts[gi]
                    rel = jnp.where((rel >= 0) & (rel < counts[gi]), rel, spare)
                    high, low = split(block_of(table, m))
                    right_high[gi, rel, ci] = high
                    right_low[gi, rel, ci] = low
                    return carry

                lax.fori_loop(0, table.shape[0] // 128, right_body, 0, unroll=4)
                first += table.shape[0] // 128

    def rights(ref, gi, at):
        return jnp.concatenate(
            [ref[gi, at + j].reshape(128 * depth, 128) for j in range(4)], axis=1
        )

    for copy in left_copies:
        copy.wait()
    lefts_of = []
    for gi in range(count):
        left = [left_held[gi, ci].reshape(rows * 128, 256) for ci in range(depth)]
        highs = [part[:, :128] for part in left]
        lows = [part[:, 128:] for part in left]
        lefts_of.append(highs + lows + highs)

    edges = sorted({0, WINDOW} | set(starts) | {s + c for s, c in zip(starts, counts)})
    for first, last in zip(edges, edges[1:]):
        active = [gi for gi in range(count) if starts[gi] <= first and last <= starts[gi] + counts[gi]]
        if not active:
            clear(dense, first, last)
            continue
        left = jnp.concatenate([part for gi in active for part in lefts_of[gi]], axis=1)

        def body(q, carry, active=active, left=left):
            right = []
            for gi in active:
                rh = rights(right_high, gi, 4 * q - starts[gi])
                right += [rh, rh, rights(right_low, gi, 4 * q - starts[gi])]
            out = jnp.dot(left, jnp.concatenate(right, axis=0), preferred_element_type=F32)
            for j in range(4):
                dense[4 * q + j] = out[:, 128 * j : 128 * j + 128].reshape(rows, 128, 128)
            return carry

        lax.fori_loop(first // 4, last // 4, body, 0, unroll=2)
    for copy in acc_copies:
        copy.wait()
    each, kept_cols = outs[0].shape[:2]
    leaving = []
    for which in (1, 0):
        side = core if which == 0 else 1 - core
        for row in range(each * portions):
            source = side * each * portions + row if by_rows else row
            at_row = 2 * side + row0 + row if by_rows else row0 + row
            at_col = 0 if by_rows else kept_cols * side
            portion = which * portions + row // each
            own, sum_in = outs[portion].at[row % each], acc[which].at[row] if acc else None

            def out_body(y, carry, own=own, sum_in=sum_in, source=source, at_row=at_row, at_col=at_col):
                value = dense[wrap(outcols[at_row, at_col + y] - base, total), source]
                own[y] = value if sum_in is None else value + sum_in[y]
                return carry

            lax.fori_loop(0, kept_cols, out_body, 0, unroll=4)
            if not straight:
                leaving.append(start(own, results[portion].at[row % each]))
    for copy in leaving:
        copy.wait()


SMEM = pl.BlockSpec(memory_space=pltpu.SMEM)
VMEM = pl.BlockSpec(memory_space=pltpu.VMEM)
HERE = pl.BlockSpec(memory_space=pl.ANY)
PARAMS = pltpu.CompilerParams(vmem_limit_bytes=60 << 20)


def stage(name, gs, crs, by_rows, part, total, meta, outcols, patterns, left, tables, acc, col0, portions=1):
    if by_rows:
        starts, counts = [4 * (g + 2) for g in gs], [20] * len(gs)
        out = (2 if part is None else 1, outcols.shape[1], 128, 128)
        row0, rows = part or 0, 2 * out[0]
    else:
        starts, counts = [max(0, 4 * g) for g in gs], [WINDOW - 4 * abs(g) for g in gs]
        out = (4 if part is None else 2, outcols.shape[1] // 2, 128, 128)
        row0, rows = 2 * (part or 0), out[0]
    tables = [tables[g][c] for g in gs for c in crs]
    kernel = functools.partial(
        stage_kernel, gs, crs, [len(t) for t in tables], starts, counts, total, by_rows, row0, col0, bool(acc), portions
    )
    shape = jax.ShapeDtypeStruct((out[0] // portions,) + out[1:], F32)
    blocks = [piece for table in tables for piece in table]
    if part is not None:
        blocks = [pltpu.with_memory_space_constraint(b, pltpu.VMEM) for b in blocks]
        acc = [pltpu.with_memory_space_constraint(a, pltpu.VMEM) for a in acc]
    straight = portions == 2 or part is not None
    window = max(counts)
    wide = pltpu.VMEM((len(gs), window + 1, len(crs), 128, 128), BF16)
    scratch = [
        wide,
        wide,
        pltpu.VMEM((WINDOW, rows, 128, 128), F32),
        pltpu.VMEM((len(gs), len(crs), rows, 128, 256), BF16),
    ]
    if part is None:
        held = [pltpu.VMEM((b.shape[0] // 128 * 128, 128), F32) for b in blocks]
        held += [pltpu.VMEM(a.shape, F32) for a in acc]
    else:
        held = []
    if not straight:
        held += [pltpu.VMEM(shape.shape, F32)] * (2 * portions)
    used = sum(math.prod(ref.shape) * jnp.dtype(ref.dtype).itemsize for ref in scratch + held)
    copies = len(blocks) + len(gs) * len(crs) + len(acc) + 2 * out[0]
    return pl.pallas_call(
        kernel,
        name=name,
        out_shape=[pltpu.VMEM(shape.shape, F32) if straight else shape] * (2 * portions),
        in_specs=[SMEM] * (2 + len(gs)) + [HERE] + [HERE if part is None else VMEM] * (len(blocks) + len(acc)),
        out_specs=[VMEM if straight else HERE] * (2 * portions),
        scratch_shapes=scratch + [pltpu.SemaphoreType.DMA((copies,))] + held,
        compiler_params=pltpu.CompilerParams(vmem_limit_bytes=used + (6 << 20)),
        cost_estimate=pl.CostEstimate(flops=0, transcendentals=0, bytes_accessed=0),
    )(
        meta, outcols, *[patterns[g] for g in gs], left[0 if part is None else 1 + part], *blocks, *acc
    )


def left_call(kernel, name, scalars, arrays):
    out = jax.ShapeDtypeStruct((5, 2, 4, 128, 256), BF16)
    last = jax.ShapeDtypeStruct((2, 1, 2, 128, 256), BF16)
    return pl.pallas_call(
        kernel,
        name=name,
        out_shape=[out, last, last],
        in_specs=[SMEM] * len(scalars) + [VMEM] * len(arrays),
        out_specs=[VMEM] * 3,
        compiler_params=PARAMS,
        cost_estimate=pl.CostEstimate(
            flops=0, transcendentals=0, bytes_accessed=0
        ),
    )(*scalars, *arrays)


def halo(own, after_first, before_last):
    first, last = ({g: ring(row, -g) for g in (-1, 1)} for row in own)
    near = after_first(first[-1], first[1])
    first[-2], first[2] = ring(near[0], 1), ring(near[1], -1)
    near = before_last(last[-1], last[1])
    last[-2], last[2] = ring(near[0], 1), ring(near[1], -1)
    tables = {g: [(first[g],), (last[g],)] for g in (-2, -1, 1, 2)}
    tables[0] = [(row,) for row in own]
    return tables


def shards(margin_blocks, margin_cols, factor_blocks, factor_cols, product_cols, metric_cols):
    total = factor_blocks.shape[0] * lax.axis_size("rows")
    position = lax.axis_index("rows")
    core = lax.axis_index("rep")
    meta = jnp.stack([position, core]).astype(jnp.int32)
    slots = factor_cols.shape[1]
    pattern = lax.dynamic_slice_in_dim(jnp.concatenate([factor_cols, product_cols], axis=1), 2 * core, 2, 0)
    own = [
        lax.dynamic_index_in_dim(factor_blocks, 2 * core + c, 0, keepdims=False).reshape(slots * 128, 128)
        for c in range(2)
    ]
    columns = jnp.pad(pattern.astype(F32), ((0, 6), (0, 128 - pattern.shape[1])))
    own[0] = jnp.concatenate([own[0], columns], axis=0)
    margin_left = left_call(
        functools.partial(margin_left_kernel, total), "margin_left",
        [meta, margin_cols, swap(margin_cols)], [margin_blocks, swap(margin_blocks)],
    )

    def after_margin(below, above):
        return lax.optimization_barrier((below, above, margin_left))[:2]

    factors = halo(own, after_margin, lambda below, above: (below, above))
    patterns = {0: pattern}
    for g in (-2, -1, 1, 2):
        patterns[g] = factors[g][0][0][slots * 128 : slots * 128 + 2, : pattern.shape[1]].astype(jnp.int32)
    part = lambda name, gs, crs, which, acc: stage(
        name, gs, crs, True, which, total, meta, product_cols, patterns, margin_left, factors, acc, 0,
        2 if gs == (-2, 2) and which is None else 1,
    )
    acc = part("product_near", (0, -1, 1), (0, 1), None, ())
    acc = part("product_far0", (-2, 2), (0,), None, acc)
    finals = [part("product_far1", (-2, 2), (1,), which, acc[which::2]) for which in range(2)]
    rows = [(kept + swap(sent))[0] for kept, sent in finals]
    both = jnp.stack(rows)
    rows = [row.reshape(-1, 128) for row in rows]
    half = both.shape[1] // 2
    mine = lax.dynamic_slice_in_dim(both, core * half, half, 1)
    theirs = swap(lax.dynamic_slice_in_dim(both, (1 - core) * half, half, 1))
    low, high = jnp.where(core == 0, mine, theirs), jnp.where(core == 0, theirs, mine)
    made = [jnp.concatenate([low, high], axis=0)]
    blocks = [factors[g][c] for g in range(-2, 3) for c in range(2)]
    factor_left = left_call(
        functools.partial(factor_left_kernel, [len(b) for b in blocks], total), "factor_left",
        [meta] + [patterns[g] for g in range(-2, 3)], [piece for b in blocks for piece in b],
    )
    products = {0: [(row,) for row in rows]}
    part = lambda name, gs, crs, which, acc: stage(
        name, gs, crs, False, which, total, meta, metric_cols, patterns, factor_left, products, acc, slots,
        2 if gs == (-2, 2) and which is None else 1,
    )
    own_acc = part("metric_own", (0,), (0, 1), None, ())

    def after_own(below, above):
        return lax.optimization_barrier((below, above, tuple(own_acc)))[:2]

    def finish_product(below, above):
        below, above, made[0] = lax.optimization_barrier((below, above, made[0]))
        return below, above

    products = halo(rows, after_own, finish_product)
    acc = part("metric_near", (-1, 1), (0, 1), None, own_acc)
    acc = part("metric_far0", (-2, 2), (0,), None, acc)
    finals = [part("metric_far1", (-2, 2), (1,), which, acc[which::2]) for which in range(2)]
    metric = jnp.concatenate([kept + swap(sent) for kept, sent in finals], axis=0)
    return (made[0], metric)


def solution(mesh):
    return jax.shard_map(
        shards,
        mesh=mesh,
        in_specs=(
            P("rows", "rep", None, None),
            P("rows", "rep"),
            P("rows", None, None, None),
            P("rows", None),
            P("rows", None),
            P("rows", None),
        ),
        out_specs=(P("rows", "rep", None, None), P("rows", "rep", None, None)),
        check_vma=False,
    )
```

```python
import functools
import math

import jax
import jax.numpy as jnp
from jax import lax
from jax.experimental import pallas as pl
from jax.experimental.pallas import tpu as pltpu
from jax.sharding import PartitionSpec as P

F32 = jnp.float32
BF16 = jnp.bfloat16
WINDOW = 36


def ring(array, by):
    devices = lax.axis_size("rows")
    return lax.ppermute(array, "rows", [(i, (i + by) % devices) for i in range(devices)])


def swap(array):
    return lax.ppermute(array, "rep", [(0, 1), (1, 0)])


def split(block):
    high = block.astype(BF16)
    return high, (block - high.astype(F32)).astype(BF16)


def block_of(table, index):
    return table[pl.ds(pl.multiple_of(index * 128, 128), 128), :]


def wrap(index, total):
    if total & (total - 1) == 0:
        return jnp.bitwise_and(index, total - 1)
    return lax.rem(index + total, total)


def clear(ref, first=0, last=None):
    zero = jnp.zeros(ref.shape[1:], ref.dtype)

    def body(i, carry):
        ref[i] = zero
        return carry

    lax.fori_loop(first, ref.shape[0] if last is None else last, body, 0, unroll=4)


def copy_last(out, parts, row_of):
    for part, ref in enumerate(parts):
        for gi, group in enumerate((0, 4)):
            for row in range(ref.shape[2]):
                ref[gi, 0, row] = out[group, 1, row_of(part, row)]


def margin_left_kernel(total, meta, cols_a, cols_b, table_a, table_b, out, part_a, part_b):
    position, core = meta[0], meta[1]
    for group in range(5):
        for c in range(2):
            clear(out.at[group, c])
    first = 4 * position - 8
    for cols, table in ((cols_a, table_a), (cols_b, table_b)):
        for row in range(4):

            def body(k, carry, cols=cols, table=table, row=row):
                rel = wrap(cols[row, k] - first, total)
                within = jnp.bitwise_and(rel, 3) - 2 * core

                @pl.when((within >= 0) & (within < 2))
                def _():
                    group = lax.shift_right_logical(rel, 2)
                    high, low = split(table[row, k])
                    out[group, within, row, :, :128] = high
                    out[group, within, row, :, 128:] = low

                return carry

            lax.fori_loop(0, table.shape[1], body, 0)
    copy_last(out, (part_a, part_b), lambda part, row: 2 * row + part)


def factor_left_kernel(pieces, total, meta, *refs):
    patterns, refs = refs[:5], refs[5:]
    out, part_a, part_b = refs[-3:]
    tables, refs = [], list(refs[:-3])
    for number in pieces:
        tables.append([refs.pop(0) for _ in range(number)])
    position = meta[0]
    for group in range(5):
        for c in range(2):
            clear(out.at[group, c])
            cols, first = patterns[group], 0
            for table in tables[2 * group + c]:

                def body(m, carry, cols=cols, table=table, group=group, c=c, first=first):
                    rel = wrap(cols[c, first + m] - 4 * position, total)

                    @pl.when(rel < 4)
                    def _():
                        high, low = split(block_of(table, m).T)
                        out[group, c, rel, :, :128] = high
                        out[group, c, rel, :, 128:] = low

                    return carry

                lax.fori_loop(0, table.shape[0] // 128, body, 0)
                first += table.shape[0] // 128
    copy_last(out, (part_a, part_b), lambda part, row: 3 * part + row)


def stage_kernel(gs, crs, pieces, starts, counts, total, by_rows, row0, col0, has_acc, portions, *refs):
    count, depth = len(gs), len(crs)
    meta, outcols = refs[:2]
    patterns = refs[2 : 2 + count]
    refs = refs[2 + count :]
    lefts, refs = refs[0], list(refs[1:])
    direct = lefts.shape[0] != 5
    sources = [refs.pop(0) for _ in range(sum(pieces))]
    acc_sources = [refs.pop(0) for _ in range(2 if has_acc else 0)]
    results = [refs.pop(0) for _ in range(2 * len(portions))]
    straight = len(portions) == 2 or direct
    right_high, right_low, dense, left_held, sems = refs[:5]
    refs = refs[5:]
    held = sources if direct else [refs.pop(0) for _ in sources]
    acc = acc_sources if direct else [refs.pop(0) for _ in acc_sources]
    outs = results if straight else refs
    copies = []

    def start(source, target):
        copies.append(pltpu.make_async_copy(source, target, sems.at[len(copies)]))
        copies[-1].start()
        return copies[-1]

    arriving = [None if direct else start(source.at[pl.ds(0, target.shape[0])], target) for source, target in zip(sources, held)]
    left_copies = []
    for gi, g in enumerate(gs):
        for ci, c in enumerate(crs):
            source = lefts.at[g + 2, c] if lefts.shape[0] == 5 else lefts.at[gi, 0]
            left_copies.append(start(source, left_held.at[gi, ci]))
    acc_copies = [] if direct else [start(source, target) for source, target in zip(acc_sources, acc)]
    tables, held = [], list(zip(held, arriving))
    for number in pieces:
        tables.append([held.pop(0) for _ in range(number)])
    core = meta[1]
    base = 4 * meta[0] - 16
    rows = dense.shape[1]
    spare = right_high.shape[1] - 1
    for gi in range(count):
        clear(right_high.at[gi], 0, counts[gi])
        clear(right_low.at[gi], 0, counts[gi])
    for gi in range(count):
        for ci, c in enumerate(crs):
            cols, first = patterns[gi], col0
            for table, copy in tables[gi * depth + ci]:
                if copy is not None:
                    copy.wait()

                def right_body(m, carry, gi=gi, ci=ci, c=c, cols=cols, table=table, first=first):
                    rel = wrap(cols[c, first + m] - base, total) - starts[gi]
                    rel = jnp.where((rel >= 0) & (rel < counts[gi]), rel, spare)
                    high, low = split(block_of(table, m))
                    right_high[gi, rel, ci] = high
                    right_low[gi, rel, ci] = low
                    return carry

                lax.fori_loop(0, table.shape[0] // 128, right_body, 0, unroll=4)
                first += table.shape[0] // 128

    def rights(ref, gi, at):
        return jnp.concatenate(
            [ref[gi, at + j].reshape(128 * depth, 128) for j in range(4)], axis=1
        )

    for copy in left_copies:
        copy.wait()
    lefts_of = []
    for gi in range(count):
        left = [left_held[gi, ci].reshape(rows * 128, 256) for ci in range(depth)]
        highs = [part[:, :128] for part in left]
        lows = [part[:, 128:] for part in left]
        lefts_of.append(highs + lows + highs)

    edges = sorted({0, WINDOW} | set(starts) | {s + c for s, c in zip(starts, counts)})
    for first, last in zip(edges, edges[1:]):
        active = [gi for gi in range(count) if starts[gi] <= first and last <= starts[gi] + counts[gi]]
        if not active:
            clear(dense, first, last)
            continue
        left = jnp.concatenate([part for gi in active for part in lefts_of[gi]], axis=1)

        def body(q, carry, active=active, left=left):
            right = []
            for gi in active:
                rh = rights(right_high, gi, 4 * q - starts[gi])
                right += [rh, rh, rights(right_low, gi, 4 * q - starts[gi])]
            out = jnp.dot(left, jnp.concatenate(right, axis=0), preferred_element_type=F32)
            for j in range(4):
                dense[4 * q + j] = out[:, 128 * j : 128 * j + 128].reshape(rows, 128, 128)
            return carry

        lax.fori_loop(first // 4, last // 4, body, 0, unroll=2)
    for copy in acc_copies:
        copy.wait()
    kept_cols = outs[0].shape[1]
    places = [(portion, row) for portion, number in enumerate(portions) for row in range(number)]
    leaving = []
    for which in (1, 0):
        side = core if which == 0 else 1 - core
        for row, (portion, local) in enumerate(places):
            source = side * len(places) + row if by_rows else row
            at_row = 2 * side + row0 + row if by_rows else row0 + row
            at_col = 0 if by_rows else kept_cols * side
            portion = which * len(portions) + portion
            own, sum_in = outs[portion].at[local], acc[which].at[row] if acc else None

            def out_body(y, carry, own=own, sum_in=sum_in, source=source, at_row=at_row, at_col=at_col):
                value = dense[wrap(outcols[at_row, at_col + y] - base, total), source]
                own[y] = value if sum_in is None else value + sum_in[y]
                return carry

            lax.fori_loop(0, kept_cols, out_body, 0, unroll=4)
            if not straight:
                leaving.append(start(own, results[portion].at[local]))
    for copy in leaving:
        copy.wait()


SMEM = pl.BlockSpec(memory_space=pltpu.SMEM)
VMEM = pl.BlockSpec(memory_space=pltpu.VMEM)
HERE = pl.BlockSpec(memory_space=pl.ANY)
PARAMS = pltpu.CompilerParams(vmem_limit_bytes=60 << 20)


def stage(name, gs, crs, by_rows, part, total, meta, outcols, patterns, left, tables, acc, col0, halves=None):
    if by_rows:
        starts, counts = [4 * (g + 2) for g in gs], [20] * len(gs)
        out = (2 if part is None else 1, outcols.shape[1], 128, 128)
        row0, rows = part or 0, 2 * out[0]
    else:
        starts, counts = [max(0, 4 * g) for g in gs], [WINDOW - 4 * abs(g) for g in gs]
        out = ((3, 1, 4)[2 if part is None else part], outcols.shape[1] // 2, 128, 128)
        row0, rows = 3 * (part or 0), out[0]
    portions = ((1, 1) if by_rows else (3, 1)) if halves else (out[0],)
    tables = [tables[g][c] for g in gs for c in crs]
    kernel = functools.partial(
        stage_kernel, gs, crs, [len(t) for t in tables], starts, counts, total, by_rows, row0, col0, bool(acc), portions
    )
    shapes = [(number,) + out[1:] for number in portions] * 2
    blocks = [piece for table in tables for piece in table]
    if part is not None:
        blocks = [pltpu.with_memory_space_constraint(b, pltpu.VMEM) for b in blocks]
        acc = [pltpu.with_memory_space_constraint(a, pltpu.VMEM) for a in acc]
    straight = halves or part is not None
    window = max(counts)
    wide = pltpu.VMEM((len(gs), window + 1, len(crs), 128, 128), BF16)
    scratch = [
        wide,
        wide,
        pltpu.VMEM((WINDOW, rows, 128, 128), F32),
        pltpu.VMEM((len(gs), len(crs), rows, 128, 256), BF16),
    ]
    if part is None:
        held = [pltpu.VMEM((b.shape[0] // 128 * 128, 128), F32) for b in blocks]
        held += [pltpu.VMEM(a.shape, F32) for a in acc]
    else:
        held = []
    if not straight:
        held += [pltpu.VMEM(shape, F32) for shape in shapes]
    used = sum(math.prod(ref.shape) * jnp.dtype(ref.dtype).itemsize for ref in scratch + held)
    copies = len(blocks) + len(gs) * len(crs) + len(acc) + 2 * out[0]
    return pl.pallas_call(
        kernel,
        name=name,
        out_shape=[pltpu.VMEM(shape, F32) if straight else jax.ShapeDtypeStruct(shape, F32) for shape in shapes],
        in_specs=[SMEM] * (2 + len(gs)) + [HERE] + [HERE if part is None else VMEM] * (len(blocks) + len(acc)),
        out_specs=[VMEM if straight else HERE] * len(shapes),
        scratch_shapes=scratch + [pltpu.SemaphoreType.DMA((copies,))] + held,
        compiler_params=pltpu.CompilerParams(vmem_limit_bytes=used + (6 << 20)),
        cost_estimate=pl.CostEstimate(flops=0, transcendentals=0, bytes_accessed=0),
    )(
        meta, outcols, *[patterns[g] for g in gs], left[0 if part is None else 1 + part], *blocks, *acc
    )


def left_call(kernel, name, scalars, arrays, parts):
    out = jax.ShapeDtypeStruct((5, 2, 4, 128, 256), BF16)
    last = [jax.ShapeDtypeStruct((2, 1, rows, 128, 256), BF16) for rows in parts]
    return pl.pallas_call(
        kernel,
        name=name,
        out_shape=[out, *last],
        in_specs=[SMEM] * len(scalars) + [VMEM] * len(arrays),
        out_specs=[VMEM] * 3,
        compiler_params=PARAMS,
        cost_estimate=pl.CostEstimate(
            flops=0, transcendentals=0, bytes_accessed=0
        ),
    )(*scalars, *arrays)


def halo(own, after_first, before_last):
    first, last = ({g: ring(row, -g) for g in (-1, 1)} for row in own)
    near = after_first(first[-1], first[1])
    first[-2], first[2] = ring(near[0], 1), ring(near[1], -1)
    near = before_last(last[-1], last[1])
    last[-2], last[2] = ring(near[0], 1), ring(near[1], -1)
    tables = {g: [(first[g],), (last[g],)] for g in (-2, -1, 1, 2)}
    tables[0] = [(row,) for row in own]
    return tables


def shards(margin_blocks, margin_cols, factor_blocks, factor_cols, product_cols, metric_cols):
    total = factor_blocks.shape[0] * lax.axis_size("rows")
    position = lax.axis_index("rows")
    core = lax.axis_index("rep")
    meta = jnp.stack([position, core]).astype(jnp.int32)
    slots = factor_cols.shape[1]
    pattern = lax.dynamic_slice_in_dim(jnp.concatenate([factor_cols, product_cols], axis=1), 2 * core, 2, 0)
    own = [
        lax.dynamic_index_in_dim(factor_blocks, 2 * core + c, 0, keepdims=False).reshape(slots * 128, 128)
        for c in range(2)
    ]
    columns = jnp.pad(pattern.astype(F32), ((0, 6), (0, 128 - pattern.shape[1])))
    own[0] = jnp.concatenate([own[0], columns], axis=0)
    margin_left = left_call(
        functools.partial(margin_left_kernel, total), "margin_left",
        [meta, margin_cols, swap(margin_cols)], [margin_blocks, swap(margin_blocks)], (2, 2),
    )

    def after_margin(below, above):
        return lax.optimization_barrier((below, above, margin_left))[:2]

    factors = halo(own, after_margin, lambda below, above: (below, above))
    patterns = {0: pattern}
    for g in (-2, -1, 1, 2):
        patterns[g] = factors[g][0][0][slots * 128 : slots * 128 + 2, : pattern.shape[1]].astype(jnp.int32)
    part = lambda name, gs, crs, which, acc: stage(
        name, gs, crs, True, which, total, meta, product_cols, patterns, margin_left, factors, acc, 0,
        gs == (-2, 2) and which is None,
    )
    acc = part("product_near", (0, -1, 1), (0, 1), None, ())
    acc = part("product_far0", (-2, 2), (0,), None, acc)
    finals = [part("product_far1", (-2, 2), (1,), which, acc[which::2]) for which in range(2)]
    rows = [(kept + swap(sent))[0] for kept, sent in finals]
    both = jnp.stack(rows)
    rows = [row.reshape(-1, 128) for row in rows]
    half = both.shape[1] // 2
    mine = lax.dynamic_slice_in_dim(both, core * half, half, 1)
    theirs = swap(lax.dynamic_slice_in_dim(both, (1 - core) * half, half, 1))
    low, high = jnp.where(core == 0, mine, theirs), jnp.where(core == 0, theirs, mine)
    made = [jnp.concatenate([low, high], axis=0)]
    blocks = [factors[g][c] for g in range(-2, 3) for c in range(2)]
    factor_left = left_call(
        functools.partial(factor_left_kernel, [len(b) for b in blocks], total), "factor_left",
        [meta] + [patterns[g] for g in range(-2, 3)], [piece for b in blocks for piece in b], (3, 1),
    )
    products = {0: [(row,) for row in rows]}
    part = lambda name, gs, crs, which, acc: stage(
        name, gs, crs, False, which, total, meta, metric_cols, patterns, factor_left, products, acc, slots,
        gs == (-2, 2) and which is None,
    )
    own_acc = part("metric_own", (0,), (0, 1), None, ())

    def after_own(below, above):
        return lax.optimization_barrier((below, above, tuple(own_acc)))[:2]

    def finish_product(below, above):
        below, above, made[0] = lax.optimization_barrier((below, above, made[0]))
        return below, above

    products = halo(rows, after_own, finish_product)
    acc = part("metric_near", (-1, 1), (0, 1), None, own_acc)
    acc = part("metric_far0", (-2, 2), (0,), None, acc)
    finals = [part("metric_far1", (-2, 2), (1,), which, acc[which::2]) for which in range(2)]
    first, last = [kept + swap(sent) for kept, sent in finals]
    metric = lax.optimization_barrier(jnp.pad(first, ((0, last.shape[0]), (0, 0), (0, 0), (0, 0))))
    metric = lax.dynamic_update_slice_in_dim(metric, last, first.shape[0], 0)
    return (made[0], metric)


def solution(mesh):
    return jax.shard_map(
        shards,
        mesh=mesh,
        in_specs=(
            P("rows", "rep", None, None),
            P("rows", "rep"),
            P("rows", None, None, None),
            P("rows", None),
            P("rows", None),
            P("rows", None),
        ),
        out_specs=(P("rows", "rep", None, None), P("rows", "rep", None, None)),
        check_vma=False,
    )
```

```python
import functools
import math

import jax
import jax.numpy as jnp
from jax import lax
from jax.experimental import pallas as pl
from jax.experimental.pallas import tpu as pltpu
from jax.sharding import PartitionSpec as P

F32 = jnp.float32
BF16 = jnp.bfloat16
WINDOW = 36


def ring(array, by):
    devices = lax.axis_size("rows")
    return lax.ppermute(array, "rows", [(i, (i + by) % devices) for i in range(devices)])


def swap(array):
    return lax.ppermute(array, "rep", [(0, 1), (1, 0)])


def split(block):
    high = block.astype(BF16)
    return high, (block - high.astype(F32)).astype(BF16)


def block_of(table, index):
    return table[pl.ds(pl.multiple_of(index * 128, 128), 128), :]


def wrap(index, total):
    if total & (total - 1) == 0:
        return jnp.bitwise_and(index, total - 1)
    return lax.rem(index + total, total)


def clear(ref, first=0, last=None):
    zero = jnp.zeros(ref.shape[1:], ref.dtype)

    def body(i, carry):
        ref[i] = zero
        return carry

    lax.fori_loop(first, ref.shape[0] if last is None else last, body, 0, unroll=4)


def copy_last(out, parts, row_of):
    for part, ref in enumerate(parts):
        for gi, group in enumerate((0, 4)):
            for row in range(ref.shape[2]):
                ref[gi, 0, row] = out[group, 1, row_of(part, row)]


def margin_left_kernel(total, meta, cols_a, cols_b, table_a, table_b, out, part_a, part_b):
    position, core = meta[0], meta[1]
    for group in range(5):
        for c in range(2):
            clear(out.at[group, c])
    first = 4 * position - 8
    for cols, table in ((cols_a, table_a), (cols_b, table_b)):
        for row in range(4):

            def body(k, carry, cols=cols, table=table, row=row):
                rel = wrap(cols[row, k] - first, total)
                within = jnp.bitwise_and(rel, 3) - 2 * core

                @pl.when((within >= 0) & (within < 2))
                def _():
                    group = lax.shift_right_logical(rel, 2)
                    high, low = split(table[row, k])
                    out[group, within, row, :, :128] = high
                    out[group, within, row, :, 128:] = low

                return carry

            lax.fori_loop(0, table.shape[1], body, 0)
    copy_last(out, (part_a, part_b), lambda part, row: 2 * row + part)


def factor_left_kernel(pieces, total, meta, *refs):
    patterns, refs = refs[:5], refs[5:]
    out, part_a, part_b = refs[-3:]
    tables, refs = [], list(refs[:-3])
    for number in pieces:
        tables.append([refs.pop(0) for _ in range(number)])
    position = meta[0]
    for group in range(5):
        for c in range(2):
            clear(out.at[group, c])
            cols, first = patterns[group], 0
            for table in tables[2 * group + c]:

                def body(m, carry, cols=cols, table=table, group=group, c=c, first=first):
                    rel = wrap(cols[c, first + m] - 4 * position, total)

                    @pl.when(rel < 4)
                    def _():
                        high, low = split(block_of(table, m).T)
                        out[group, c, rel, :, :128] = high
                        out[group, c, rel, :, 128:] = low

                    return carry

                lax.fori_loop(0, table.shape[0] // 128, body, 0)
                first += table.shape[0] // 128
    copy_last(out, (part_a, part_b), lambda part, row: 3 * part + row)


def stage_kernel(gs, crs, pieces, starts, counts, total, by_rows, row0, col0, has_acc, portions, *refs):
    count, depth = len(gs), len(crs)
    meta, outcols = refs[:2]
    patterns = refs[2 : 2 + count]
    refs = refs[2 + count :]
    lefts, refs = refs[0], list(refs[1:])
    direct = lefts.shape[0] != 5
    sources = [refs.pop(0) for _ in range(sum(pieces))]
    acc_sources = [refs.pop(0) for _ in range(2 if has_acc else 0)]
    results = [refs.pop(0) for _ in range(2 * len(portions))]
    straight = len(portions) == 2 or direct
    right_high, right_low, dense, left_held, sems = refs[:5]
    refs = refs[5:]
    held = sources if direct else [refs.pop(0) for _ in sources]
    acc = acc_sources if direct else [refs.pop(0) for _ in acc_sources]
    staged = by_rows and direct
    outs = [refs[0], results[1]] if staged else results if straight else refs
    copies = []

    def start(source, target):
        copies.append(pltpu.make_async_copy(source, target, sems.at[len(copies)]))
        copies[-1].start()
        return copies[-1]

    arriving = [None if direct else start(source.at[pl.ds(0, target.shape[0])], target) for source, target in zip(sources, held)]
    left_copies = []
    for gi, g in enumerate(gs):
        for ci, c in enumerate(crs):
            source = lefts.at[g + 2, c] if lefts.shape[0] == 5 else lefts.at[gi, 0]
            left_copies.append(start(source, left_held.at[gi, ci]))
    acc_copies = [] if direct else [start(source, target) for source, target in zip(acc_sources, acc)]
    tables, held = [], list(zip(held, arriving))
    for number in pieces:
        tables.append([held.pop(0) for _ in range(number)])
    core = meta[1]
    base = 4 * meta[0] - 16
    rows = dense.shape[1]
    spare = right_high.shape[1] - 1
    for gi in range(count):
        clear(right_high.at[gi], 0, counts[gi])
        clear(right_low.at[gi], 0, counts[gi])
    for gi in range(count):
        for ci, c in enumerate(crs):
            cols, first = patterns[gi], col0
            for table, copy in tables[gi * depth + ci]:
                if copy is not None:
                    copy.wait()

                def right_body(m, carry, gi=gi, ci=ci, c=c, cols=cols, table=table, first=first):
                    rel = wrap(cols[c, first + m] - base, total) - starts[gi]
                    rel = jnp.where((rel >= 0) & (rel < counts[gi]), rel, spare)
                    high, low = split(block_of(table, m))
                    right_high[gi, rel, ci] = high
                    right_low[gi, rel, ci] = low
                    return carry

                lax.fori_loop(0, table.shape[0] // 128, right_body, 0, unroll=4)
                first += table.shape[0] // 128

    def rights(ref, gi, at):
        return jnp.concatenate(
            [ref[gi, at + j].reshape(128 * depth, 128) for j in range(4)], axis=1
        )

    for copy in left_copies:
        copy.wait()
    lefts_of = []
    for gi in range(count):
        left = [left_held[gi, ci].reshape(rows * 128, 256) for ci in range(depth)]
        highs = [part[:, :128] for part in left]
        lows = [part[:, 128:] for part in left]
        lefts_of.append(highs + lows + highs)

    edges = sorted({0, WINDOW} | set(starts) | {s + c for s, c in zip(starts, counts)})
    for first, last in zip(edges, edges[1:]):
        active = [gi for gi in range(count) if starts[gi] <= first and last <= starts[gi] + counts[gi]]
        if not active:
            clear(dense, first, last)
            continue
        left = jnp.concatenate([part for gi in active for part in lefts_of[gi]], axis=1)

        def body(q, carry, active=active, left=left):
            right = []
            for gi in active:
                rh = rights(right_high, gi, 4 * q - starts[gi])
                right += [rh, rh, rights(right_low, gi, 4 * q - starts[gi])]
            out = jnp.dot(left, jnp.concatenate(right, axis=0), preferred_element_type=F32)
            for j in range(4):
                dense[4 * q + j] = out[:, 128 * j : 128 * j + 128].reshape(rows, 128, 128)
            return carry

        lax.fori_loop(first // 4, last // 4, body, 0, unroll=2)
    for copy in acc_copies:
        copy.wait()
    kept_cols = outs[0].shape[1]
    places = [(portion, row) for portion, number in enumerate(portions) for row in range(number)]
    leaving = []
    for which in (0, 1) if staged else (1, 0):
        side = core if which == 0 else 1 - core
        for row, (portion, local) in enumerate(places):
            source = side * len(places) + row if by_rows else row
            at_row = 2 * side + row0 + row if by_rows else row0 + row
            at_col = 0 if by_rows else kept_cols * side
            portion = which * len(portions) + portion
            own, sum_in = outs[portion].at[local], acc[which].at[row] if acc else None

            def out_body(y, carry, own=own, sum_in=sum_in, source=source, at_row=at_row, at_col=at_col):
                value = dense[wrap(outcols[at_row, at_col + y] - base, total), source]
                own[y] = value if sum_in is None else value + sum_in[y]
                return carry

            lax.fori_loop(0, kept_cols, out_body, 0, unroll=4)
            if not straight or (staged and which == 0):
                leaving.append(start(own, results[portion].at[local]))
    for copy in leaving:
        copy.wait()


SMEM = pl.BlockSpec(memory_space=pltpu.SMEM)
VMEM = pl.BlockSpec(memory_space=pltpu.VMEM)
HERE = pl.BlockSpec(memory_space=pl.ANY)
FAR = pl.BlockSpec(memory_space=pltpu.HBM)
PARAMS = pltpu.CompilerParams(vmem_limit_bytes=60 << 20)


def stage(name, gs, crs, by_rows, part, total, meta, outcols, patterns, left, tables, acc, col0, halves=None):
    if by_rows:
        starts, counts = [4 * (g + 2) for g in gs], [20] * len(gs)
        out = (2 if part is None else 1, outcols.shape[1], 128, 128)
        row0, rows = part or 0, 2 * out[0]
    else:
        starts, counts = [max(0, 4 * g) for g in gs], [WINDOW - 4 * abs(g) for g in gs]
        out = ((3, 1, 4)[2 if part is None else part], outcols.shape[1] // 2, 128, 128)
        row0, rows = 3 * (part or 0), out[0]
    portions = ((1, 1) if by_rows else (3, 1)) if halves else (out[0],)
    tables = [tables[g][c] for g in gs for c in crs]
    kernel = functools.partial(
        stage_kernel, gs, crs, [len(t) for t in tables], starts, counts, total, by_rows, row0, col0, bool(acc), portions
    )
    shapes = [(number,) + out[1:] for number in portions] * 2
    blocks = [piece for table in tables for piece in table]
    if part is not None:
        blocks = [pltpu.with_memory_space_constraint(b, pltpu.VMEM) for b in blocks]
        acc = [pltpu.with_memory_space_constraint(a, pltpu.VMEM) for a in acc]
    straight = halves or part is not None
    window = max(counts)
    wide = pltpu.VMEM((len(gs), window + 1, len(crs), 128, 128), BF16)
    scratch = [
        wide,
        wide,
        pltpu.VMEM((WINDOW, rows, 128, 128), F32),
        pltpu.VMEM((len(gs), len(crs), rows, 128, 256), BF16),
    ]
    if part is None:
        held = [pltpu.VMEM((b.shape[0] // 128 * 128, 128), F32) for b in blocks]
        held += [pltpu.VMEM(a.shape, F32) for a in acc]
    else:
        held = []
    staged = by_rows and part is not None
    in_vmem = [straight and not (staged and i == 0) for i in range(len(shapes))]
    if staged:
        held += [pltpu.VMEM(shapes[0], F32)]
    if not straight:
        held += [pltpu.VMEM(shape, F32) for shape in shapes]
    used = sum(math.prod(ref.shape) * jnp.dtype(ref.dtype).itemsize for ref in scratch + held)
    copies = len(blocks) + len(gs) * len(crs) + len(acc) + 2 * out[0]
    return pl.pallas_call(
        kernel,
        name=name,
        out_shape=[
            (pltpu.VMEM if inside else pltpu.HBM)(shape, F32) if straight else jax.ShapeDtypeStruct(shape, F32)
            for shape, inside in zip(shapes, in_vmem)
        ],
        in_specs=[SMEM] * (2 + len(gs)) + [HERE] + [HERE if part is None else VMEM] * (len(blocks) + len(acc)),
        out_specs=[VMEM if inside else FAR if straight else HERE for inside in in_vmem],
        scratch_shapes=scratch + [pltpu.SemaphoreType.DMA((copies,))] + held,
        compiler_params=pltpu.CompilerParams(vmem_limit_bytes=used + (6 << 20)),
        cost_estimate=pl.CostEstimate(flops=0, transcendentals=0, bytes_accessed=0),
    )(
        meta, outcols, *[patterns[g] for g in gs], left[0 if part is None else 1 + part], *blocks, *acc
    )


def left_call(kernel, name, scalars, arrays, parts):
    out = jax.ShapeDtypeStruct((5, 2, 4, 128, 256), BF16)
    last = [jax.ShapeDtypeStruct((2, 1, rows, 128, 256), BF16) for rows in parts]
    return pl.pallas_call(
        kernel,
        name=name,
        out_shape=[out, *last],
        in_specs=[SMEM] * len(scalars) + [VMEM] * len(arrays),
        out_specs=[VMEM] * 3,
        compiler_params=PARAMS,
        cost_estimate=pl.CostEstimate(
            flops=0, transcendentals=0, bytes_accessed=0
        ),
    )(*scalars, *arrays)


def halo(own, after_first, before_last):
    first, last = ({g: ring(row, -g) for g in (-1, 1)} for row in own)
    near = after_first(first[-1], first[1])
    first[-2], first[2] = ring(near[0], 1), ring(near[1], -1)
    near = before_last(last[-1], last[1])
    last[-2], last[2] = ring(near[0], 1), ring(near[1], -1)
    tables = {g: [(first[g],), (last[g],)] for g in (-2, -1, 1, 2)}
    tables[0] = [(row,) for row in own]
    return tables


def shards(margin_blocks, margin_cols, factor_blocks, factor_cols, product_cols, metric_cols):
    total = factor_blocks.shape[0] * lax.axis_size("rows")
    position = lax.axis_index("rows")
    core = lax.axis_index("rep")
    meta = jnp.stack([position, core]).astype(jnp.int32)
    slots = factor_cols.shape[1]
    pattern = lax.dynamic_slice_in_dim(jnp.concatenate([factor_cols, product_cols], axis=1), 2 * core, 2, 0)
    own = [
        lax.dynamic_index_in_dim(factor_blocks, 2 * core + c, 0, keepdims=False).reshape(slots * 128, 128)
        for c in range(2)
    ]
    columns = jnp.pad(pattern.astype(F32), ((0, 6), (0, 128 - pattern.shape[1])))
    own[0] = jnp.concatenate([own[0], columns], axis=0)
    margin_left = left_call(
        functools.partial(margin_left_kernel, total), "margin_left",
        [meta, margin_cols, swap(margin_cols)], [margin_blocks, swap(margin_blocks)], (2, 2),
    )

    def after_margin(below, above):
        return lax.optimization_barrier((below, above, margin_left))[:2]

    factors = halo(own, after_margin, lambda below, above: (below, above))
    patterns = {0: pattern}
    for g in (-2, -1, 1, 2):
        patterns[g] = factors[g][0][0][slots * 128 : slots * 128 + 2, : pattern.shape[1]].astype(jnp.int32)
    part = lambda name, gs, crs, which, acc: stage(
        name, gs, crs, True, which, total, meta, product_cols, patterns, margin_left, factors, acc, 0,
        gs == (-2, 2) and which is None,
    )
    acc = part("product_near", (0, -1, 1), (0, 1), None, ())
    acc = part("product_far0", (-2, 2), (0,), None, acc)
    finals = [part("product_far1", (-2, 2), (1,), which, acc[which::2]) for which in range(2)]
    rows = [(kept + swap(sent))[0] for kept, sent in finals]
    both = jnp.stack(rows)
    rows = [row.reshape(-1, 128) for row in rows]
    half = both.shape[1] // 2
    mine = lax.dynamic_slice_in_dim(both, core * half, half, 1)
    theirs = swap(lax.dynamic_slice_in_dim(both, (1 - core) * half, half, 1))
    low, high = jnp.where(core == 0, mine, theirs), jnp.where(core == 0, theirs, mine)
    made = [jnp.concatenate([low, high], axis=0)]
    blocks = [factors[g][c] for g in range(-2, 3) for c in range(2)]
    factor_left = left_call(
        functools.partial(factor_left_kernel, [len(b) for b in blocks], total), "factor_left",
        [meta] + [patterns[g] for g in range(-2, 3)], [piece for b in blocks for piece in b], (3, 1),
    )
    products = {0: [(row,) for row in rows]}
    part = lambda name, gs, crs, which, acc: stage(
        name, gs, crs, False, which, total, meta, metric_cols, patterns, factor_left, products, acc, slots,
        gs == (-2, 2) and which is None,
    )
    own_acc = part("metric_own", (0,), (0, 1), None, ())

    def after_own(below, above):
        return lax.optimization_barrier((below, above, tuple(own_acc)))[:2]

    def finish_product(below, above):
        below, above, made[0] = lax.optimization_barrier((below, above, made[0]))
        return below, above

    products = halo(rows, after_own, finish_product)
    acc = part("metric_near", (-1, 1), (0, 1), None, own_acc)
    acc = part("metric_far0", (-2, 2), (0,), None, acc)
    finals = [part("metric_far1", (-2, 2), (1,), which, acc[which::2]) for which in range(2)]
    first, last = [kept + swap(sent) for kept, sent in finals]
    metric = lax.optimization_barrier(jnp.pad(first, ((0, last.shape[0]), (0, 0), (0, 0), (0, 0))))
    metric = lax.dynamic_update_slice_in_dim(metric, last, first.shape[0], 0)
    return (made[0], metric)


def solution(mesh):
    return jax.shard_map(
        shards,
        mesh=mesh,
        in_specs=(
            P("rows", "rep", None, None),
            P("rows", "rep"),
            P("rows", None, None, None),
            P("rows", None),
            P("rows", None),
            P("rows", None),
        ),
        out_specs=(P("rows", "rep", None, None), P("rows", "rep", None, None)),
        check_vma=False,
    )
```
